32 devices in a mesh: ctx: 16 (over z, y, core), head: 2 (over x).
Axes of the slice: x: 2, y: 2, z: 4, core: 2. Of those that a mesh axis runs over, the one named last changes fastest.
Arguments:
- queries: bfloat16 [4096, 2048], P(('ctx', 'head')), may hold values from -24 to 24
- keys: bfloat16 [4096, 256], P(('ctx', 'head')), may hold values from -24 to 24
- values: bfloat16 [4096, 256], P(('ctx', 'head')), may hold values from -6 to 6
- d_out: bfloat16 [4096, 2048], P(('ctx', 'head')), may hold values from -6 to 6
- doc_lengths: int32 [32], replicated, may hold values from 1 to 768, 4096 in all
Outputs:
- attn_out: bfloat16 [4096, 2048], P('ctx', 'head')
- grad_queries: bfloat16 [4096, 2048], P('ctx', 'head')
- grad_keys: bfloat16 [4096, 256], P('ctx', 'head')
- grad_values: bfloat16 [4096, 256], P('ctx', 'head')
The draws below stay inside these ranges and needn't reach their ends.
Inputs may be any that keep to these rules, and one draw needn't show every extreme that they name: `doc_lengths`: the lengths sum to 4096; some document holds exactly 768 tokens.
All inputs are finite; a program needn't handle non-finite values.
Results may differ from the reference program's by a relative error of at most 0.02.
Values may be sent and summed in bfloat16 or wider, within the bound.
No kernel may reach another device: no remote copies, remote signals or barrier semaphores. Data moves between devices by JAX's collectives and lax.ppermute only.
A program may use at most 64 MiB of HBM per device.

```python
import math
import jax
import jax.numpy as jnp
import numpy as np
from jax import lax

HD = 128
GROUP = 8
KVH = 2
QH = 16
TOK_DEV = 256
TOKENS = 4096
WIN = 4
MAXDOC = 768
NDOC = 32
N_CTX = 16


def paired_draw(key):
    base = jax.random.fold_in(key, 4242)
    key_raw, key_scale, query_raw, query_scale = jax.random.split(base, 4)
    lower = math.log(0.35)
    upper = math.log(3.5)
    raw_keys = jnp.clip(jax.random.normal(key_raw, (TOKENS, KVH, HD), jnp.float32), -4.0, 4.0)
    key_rows = jnp.exp(jax.random.uniform(key_scale, (TOKENS, KVH, 1), jnp.float32, lower, upper))
    keys_all = raw_keys * key_rows
    raw_query = jnp.clip(jax.random.normal(query_raw, (TOKENS, KVH, GROUP, HD), jnp.float32), -4.0, 4.0)
    query_rows = jnp.exp(jax.random.uniform(query_scale, (TOKENS, KVH, 1, 1), jnp.float32, lower, upper))
    query_all = raw_query * query_rows
    return (query_all.reshape(TOKENS, KVH * GROUP * HD), keys_all.reshape(TOKENS, KVH * HD))


def draw_queries(key, part):
    return paired_draw(key)[0].astype(jnp.bfloat16)


def draw_keys(key, part):
    return paired_draw(key)[1].astype(jnp.bfloat16)


def block_levels(rng, extent, shards, smallest, largest):
    factor_of = 1.0
    for dim, shards_of in shards:
        draws = jax.random.uniform(jax.random.fold_in(jax.random.fold_in(rng, 6), dim), (shards_of,), jnp.float32, smallest / len(shards), largest / len(shards))
        factor_of = factor_of * jnp.repeat(jnp.exp(draws), extent[dim] // shards_of).reshape((-1,) + (1,) * (len(extent) - 1 - dim))
    return factor_of


def profile(amount, total, most, lean):
    weights = [(1 << 20) // math.isqrt(rank ** lean) + 1 for rank in range(2, amount + 1)]
    spare, counts = total - most - (amount - 1), [1] * (amount - 1)
    while spare > 0:
        free = [i for i in range(amount - 1) if counts[i] < most]
        pool, remaining = sum([weights[i] for i in free]), spare
        for i in free:
            extra = min(most - counts[i], max(1, remaining * weights[i] // pool), spare)
            counts[i] = counts[i] + extra
            spare = spare - extra
    return np.array([most] + counts)


def ragged(key, number_of, total, reach, skew):
    if number_of == 2:
        one = jax.random.randint(key, (), max(1, total - reach), min(reach, total - 1) + 1)
        return jnp.stack([one, total - one])
    sizes = jnp.asarray(profile(number_of, total, reach, skew), jnp.int32)
    twos = (number_of - 1) // 2
    donor, receiver = sizes[1:1 + 2 * twos:2], sizes[2:2 + 2 * twos:2]
    margin = jnp.minimum(donor - 1, reach - receiver)
    moved = jax.random.randint(jax.random.fold_in(key, 1), (twos,), 0, 1 << 20) % (margin + 1)
    sizes = sizes.at[1:1 + 2 * twos:2].set(donor - moved).at[2:2 + 2 * twos:2].set(receiver + moved)
    return sizes[jax.random.permutation(jax.random.fold_in(key, 2), number_of)]


def noise(rng, shape, width, limit, pieces=(), kind=jnp.bfloat16):
    factor_of = block_levels(rng, shape, pieces, -0.22, 0.18) if pieces else 1.0
    result = jax.random.normal(rng, shape, jnp.float32) * width * factor_of
    return jnp.minimum(jnp.maximum(result, -limit), limit).astype(kind)


def setup_inputs(seed: int = 0) -> dict:
    splits = jax.random.split(jax.random.key(seed), 6)
    queries = draw_queries(jax.random.fold_in(splits[5], 71), 0)
    keys = draw_keys(jax.random.fold_in(splits[5], 71), 0)
    values = noise(splits[2], (TOKENS, KVH * HD), 1.0, 6.0, ((0, 32),))
    d_out = noise(splits[3], (TOKENS, QH * HD), 1.0, 6.0, ((0, 32),))
    doc_lengths = ragged(splits[4], NDOC, TOKENS, MAXDOC, 2).astype(jnp.int32)
    return dict(queries=queries, keys=keys, values=values, d_out=d_out, doc_lengths=doc_lengths)


def token_docs(starts, positions):
    return jnp.sum((starts[None, :] <= positions[:, None]).astype(jnp.int32), axis=1)


def attend_group(query_group, key_window, value_window, grad_group, allowed, scaling):
    scores = jnp.einsum("htd,kd->htk", query_group, key_window) * scaling
    scores = jnp.where(allowed[None], scores, -jnp.inf)
    maximum = jnp.max(scores, axis=2, keepdims=True)
    totals = jnp.sum(jnp.exp(scores - maximum), axis=2, keepdims=True)
    log_total = maximum + jnp.log(totals)
    weights = jnp.exp(scores - log_total)
    rounded = lax.optimization_barrier(weights.astype(jnp.bfloat16)).astype(jnp.float32)
    outputs = jnp.einsum("htk,kd->htd", rounded, value_window).astype(jnp.bfloat16)
    deltas = jnp.sum(grad_group * outputs.astype(jnp.float32), axis=2, keepdims=True)
    grad_weights = jnp.einsum("htd,kd->htk", grad_group, value_window)
    grad_scores = lax.optimization_barrier((weights * (grad_weights - deltas)).astype(jnp.bfloat16)).astype(jnp.float32)
    grad_query = (jnp.einsum("htk,kd->htd", grad_scores, key_window) * scaling).astype(jnp.bfloat16)
    grad_key = jnp.einsum("htk,htd->kd", grad_scores, query_group) * scaling
    grad_value = jnp.einsum("htk,htd->kd", rounded, grad_group)
    return outputs, grad_query, grad_key, grad_value


def reference(queries, keys, values, d_out, doc_lengths):
    lead_rows = (WIN - 1) * TOK_DEV
    span_rows = WIN * TOK_DEV
    scaling = HD ** -0.5
    starts = jnp.cumsum(doc_lengths) - doc_lengths
    front = jnp.zeros((lead_rows, KVH * HD), jnp.float32)
    key_padded = jnp.concatenate([front, keys.astype(jnp.float32)], 0).reshape(TOKENS + lead_rows, KVH, HD)
    value_padded = jnp.concatenate([front, values.astype(jnp.float32)], 0).reshape(TOKENS + lead_rows, KVH, HD)
    query_heads = queries.astype(jnp.float32).reshape(TOKENS, KVH, GROUP, HD)
    grad_heads = d_out.astype(jnp.float32).reshape(TOKENS, KVH, GROUP, HD)

    def one_shard(carry, shard_index):
        first_row = shard_index * TOK_DEV
        query_pos = first_row + jnp.arange(TOK_DEV, dtype=jnp.int32)
        key_pos = first_row - lead_rows + jnp.arange(span_rows, dtype=jnp.int32)
        same_doc = token_docs(starts, query_pos)[:, None] == token_docs(starts, key_pos)[None, :]
        allowed = same_doc & (key_pos[None, :] <= query_pos[:, None])
        query_block = lax.dynamic_slice_in_dim(query_heads, first_row, TOK_DEV, 0).transpose(1, 2, 0, 3)
        grad_block = lax.dynamic_slice_in_dim(grad_heads, first_row, TOK_DEV, 0).transpose(1, 2, 0, 3)
        key_window = lax.dynamic_slice_in_dim(key_padded, first_row, span_rows, 0).transpose(1, 0, 2)
        value_window = lax.dynamic_slice_in_dim(value_padded, first_row, span_rows, 0).transpose(1, 0, 2)
        outputs, grad_query, grad_key, grad_value = jax.vmap(attend_group, in_axes=(0, 0, 0, 0, None, None))(
            query_block, key_window, value_window, grad_block, allowed, scaling)
        stacked = jnp.concatenate([grad_key, grad_value], axis=2).transpose(1, 0, 2)
        before = lax.dynamic_slice_in_dim(carry, first_row, span_rows, 0)
        carry = lax.dynamic_update_slice_in_dim(carry, before + stacked, first_row, 0)
        return carry, (outputs, grad_query)

    start_carry = jnp.zeros((TOKENS + lead_rows, KVH, 2 * HD), jnp.float32)
    summed, (outputs, grad_query) = lax.scan(one_shard, start_carry, jnp.arange(N_CTX, dtype=jnp.int32))
    attn_out = outputs.transpose(0, 3, 1, 2, 4).reshape(TOKENS, QH * HD)
    grad_queries = grad_query.transpose(0, 3, 1, 2, 4).reshape(TOKENS, QH * HD)
    summed = summed[lead_rows:]
    grad_keys = summed[:, :, :HD].reshape(TOKENS, KVH * HD).astype(jnp.bfloat16)
    grad_values = summed[:, :, HD:].reshape(TOKENS, KVH * HD).astype(jnp.bfloat16)
    return attn_out, grad_queries, grad_keys, grad_values
```

```python
import functools
import math

import jax
import jax.numpy as jnp
from jax import lax
from jax.experimental import pallas as pl
from jax.experimental.pallas import tpu as pltpu
from jax.sharding import PartitionSpec as P

WIN = 4
KEYS = 128
HEADS = 2
MASKED = -1e30
NT = (((1,), (1,)), ((), ()))
NN = (((1,), (0,)), ((), ()))


def dot(a, b, dims):
    return lax.dot_general(a, b, dims, preferred_element_type=jnp.float32)


def fold(x, op):
    return op(x.reshape(x.shape[0] // 8, 8, x.shape[1]), axis=0)


def attend_kernel(tiles, tile_of, flip_of, last, *refs):
    info, q_ref, do_ref = refs[:3]
    shard_refs = refs[3 : 3 + WIN]
    rest = refs[3 + WIN :]
    if last and tiles > 1:
        acc_in, _, _ = rest[:3]
        rest = rest[3:]
    else:
        acc_in = None
    out_ref, dq_ref = rest[:2]
    if last:
        own_ref = rest[2]
        far_refs = rest[3 : 2 + WIN]
        rest = rest[2 + WIN :]
    else:
        acc_out = rest[2]
        rest = rest[3:]
    k_ref, v_ref, kt_ref, vt_ref, bias_ref, s_ref, p_ref, ds_ref, acc_ref = rest

    shard = shard_refs[0].shape[0]
    hd = shard_refs[0].shape[1] // 2
    rows = q_ref.shape[0]
    lead = (WIN - 1) * shard
    blocks = bias_ref.shape[0] // KEYS
    step = pl.program_id(0)
    tile = tile_of(info)
    base = pl.multiple_of(tile * rows, KEYS)
    log2e = math.log2(math.e) / math.sqrt(hd)

    @pl.when(step == 0)
    def _():
        part = shard // tiles
        for s in range(WIN):
            for j in range(tiles):
                at = pl.multiple_of((WIN - 1 - s) * shard + (j ^ flip_of(info)) * part, 8 if part % KEYS else KEYS)
                k_ref[pl.ds(at, part), :] = shard_refs[s][j * part : (j + 1) * part, :hd]
                v_ref[pl.ds(at, part), :] = shard_refs[s][j * part : (j + 1) * part, hd:]
        for b in range(blocks):
            at = pl.ds(pl.multiple_of(base + b * KEYS, KEYS), KEYS)
            cols = slice(b * KEYS, (b + 1) * KEYS)
            kt_ref[:, cols] = k_ref[at, :].T
            vt_ref[:, cols] = v_ref[at, :].T
        first = info[0] * shard + tile * rows
        query = first + lax.broadcasted_iota(jnp.int32, (1, rows), 1)
        low = jnp.zeros((1, rows), jnp.int32)
        start = jnp.int32(0)
        for d in range(info.shape[0] - 2):
            low = jnp.where(query >= start, start, low)
            start = start + info[2 + d]
        for b in range(blocks):
            key = first - lead + b * KEYS + lax.broadcasted_iota(jnp.int32, (KEYS, rows), 0)
            ok = (key >= low) & (key <= query)
            bias_ref[b * KEYS : (b + 1) * KEYS, :] = jnp.where(ok, 0.0, MASKED)
        if acc_in is not None:
            acc_ref[...] = acc_in[...]
        else:
            acc_ref[...] = jnp.zeros_like(acc_ref)

    def block(b):
        return pl.ds(pl.multiple_of(base + b * KEYS, KEYS), KEYS)

    q = jnp.concatenate([q_ref[:, i * hd : (i + 1) * hd] for i in range(HEADS)], axis=0)
    do = jnp.concatenate([do_ref[:, i * hd : (i + 1) * hd] for i in range(HEADS)], axis=0)
    top = None
    for b in range(blocks):
        bias = bias_ref[b * KEYS : (b + 1) * KEYS, :]
        s = dot(k_ref[block(b), :], q, NT) + jnp.concatenate([bias] * HEADS, axis=1)
        s_ref[b * KEYS : (b + 1) * KEYS, :] = s
        m = fold(s, jnp.max)
        top = m if top is None else jnp.maximum(top, m)
    top = jnp.max(top, axis=0, keepdims=True)
    total = None
    for b in range(blocks):
        at = slice(b * KEYS, (b + 1) * KEYS)
        e = jnp.exp2((s_ref[at, :] - top) * log2e)
        s_ref[at, :] = e
        m = fold(e, jnp.sum)
        total = m if total is None else total + m
    inverse = 1.0 / jnp.sum(total, axis=0, keepdims=True)
    for b in range(blocks):
        at = slice(b * KEYS, (b + 1) * KEYS)
        p = s_ref[at, :] * inverse
        s_ref[at, :] = p
        p_ref[at, :] = p.astype(jnp.bfloat16)
    out = dot(vt_ref[...], p_ref[...], NN).astype(jnp.bfloat16)
    delta = jnp.sum(do.T.astype(jnp.float32) * out.astype(jnp.float32), axis=0, keepdims=True)
    for i in range(HEADS):
        out_ref[:, i * hd : (i + 1) * hd] = out[:, i * rows : (i + 1) * rows].T
    for b in range(blocks):
        at = slice(b * KEYS, (b + 1) * KEYS)
        dp = dot(v_ref[block(b), :], do, NT)
        ds = (s_ref[at, :] * (dp - delta)).astype(jnp.bfloat16)
        ds_ref[at, :] = ds
        acc_ref[block(b), :hd] += dot(ds, q, NN)
        acc_ref[block(b), hd:] += dot(p_ref[at, :], do, NN)
    dq = (dot(kt_ref[...], ds_ref[...], NN) / math.sqrt(hd)).astype(jnp.bfloat16)
    for i in range(HEADS):
        dq_ref[:, i * hd : (i + 1) * hd] = dq[:, i * rows : (i + 1) * rows].T

    @pl.when(step == pl.num_programs(0) - 1)
    def _():
        if last:
            own_ref[:, :hd] = acc_ref[lead:, :hd] / math.sqrt(hd)
            own_ref[:, hd:] = acc_ref[lead:, hd:]
            for s in range(1, WIN):
                at = slice((WIN - 1 - s) * shard, (WIN - s) * shard)
                far_refs[s - 1][:, :hd] = (acc_ref[at, :hd] / math.sqrt(hd)).astype(jnp.bfloat16)
                far_refs[s - 1][:, hd:] = acc_ref[at, hd:].astype(jnp.bfloat16)
        else:
            acc_out[...] = acc_ref[...]


def attend(info, q, do, shards, before, tiles, tile_of, flip_of, q_column):
    shard, width = shards[0].shape
    hd = width // 2
    rows = shard // tiles
    columns = HEADS * hd
    heads_columns = q_column[1]
    last = before is not None or tiles == 1
    keys = (WIN - 1) * shard + rows
    whole = pl.BlockSpec(memory_space=pltpu.VMEM)
    q_spec = pl.BlockSpec((rows, columns), lambda p, n: (0, q_column[0](n) + p))
    o_spec = pl.BlockSpec((rows, columns), lambda p, n: (tile_of(n), p))
    o_shape = jax.ShapeDtypeStruct((shard, heads_columns), jnp.bfloat16)
    acc_shape = jax.ShapeDtypeStruct((WIN * shard, width), jnp.float32)
    in_specs = [q_spec, q_spec] + [whole] * WIN
    args = [q, do, *shards]
    aliases = {}
    if before is not None:
        acc, out, dq = before
        in_specs += [whole, pl.BlockSpec(memory_space=pl.ANY), pl.BlockSpec(memory_space=pl.ANY)]
        aliases = {len(args) + 2: 0, len(args) + 3: 1}
        args += [acc, out, dq]
    if last:
        out_specs = [o_spec, o_spec] + [whole] * WIN
        out_shape = [o_shape, o_shape, jax.ShapeDtypeStruct((shard, width), jnp.float32)]
        out_shape += [jax.ShapeDtypeStruct((shard, width), jnp.bfloat16)] * (WIN - 1)
    else:
        out_specs = [o_spec, o_spec, whole]
        out_shape = [o_shape, o_shape, acc_shape]
    n = HEADS * rows
    return pl.pallas_call(
        functools.partial(attend_kernel, tiles, tile_of, flip_of, last),
        out_shape=out_shape,
        grid_spec=pltpu.PrefetchScalarGridSpec(
            num_scalar_prefetch=1,
            grid=(heads_columns // columns,),
            in_specs=in_specs,
            out_specs=out_specs,
            scratch_shapes=[
                pltpu.VMEM((WIN * shard, hd), jnp.bfloat16),
                pltpu.VMEM((WIN * shard, hd), jnp.bfloat16),
                pltpu.VMEM((hd, keys), jnp.bfloat16),
                pltpu.VMEM((hd, keys), jnp.bfloat16),
                pltpu.VMEM((keys, rows), jnp.float32),
                pltpu.VMEM((keys, n), jnp.float32),
                pltpu.VMEM((keys, n), jnp.bfloat16),
                pltpu.VMEM((keys, n), jnp.bfloat16),
                pltpu.VMEM((WIN * shard, width), jnp.float32),
            ],
        ),
        input_output_aliases=aliases,
        cost_estimate=pl.CostEstimate(
            flops=12 * keys * rows * heads_columns, transcendentals=keys * rows * heads_columns // hd, bytes_accessed=1 << 21
        ),
        name="attend_last" if last else "attend_first",
    )(info, *args)


def gather_kernel(own_ref, *refs):
    total = own_ref[...]
    for r in refs[:-2]:
        total = total + r[...].astype(jnp.float32)
    hd = refs[-1].shape[1]
    refs[-2][...] = total[:, :hd].astype(jnp.bfloat16)
    refs[-1][...] = total[:, hd:].astype(jnp.bfloat16)


def ring(value, axis, steps):
    count = lax.axis_size(axis)
    return lax.ppermute(value, axis, [(i, (i + steps) % count) for i in range(count)])


def body(queries, keys, values, d_out, doc_lengths):
    count = lax.axis_size("head")
    head = lax.axis_index("head")
    part = queries.shape[0]
    shard = count * part
    hd = keys.shape[1] // count
    group_columns = queries.shape[1] // count
    info = jnp.concatenate([jnp.stack([lax.axis_index("ctx"), head]).astype(jnp.int32), doc_lengths])
    if count == 2:
        other = 1 - head

        def columns(x, index, width):
            return lax.dynamic_slice_in_dim(x, index * width, width, 1)

        def key_value(index):
            return jnp.concatenate([columns(keys, index, hd), columns(values, index, hd)], axis=1)

        def swap(x):
            return lax.ppermute(x, "head", [(0, 1), (1, 0)])

        own = jnp.concatenate([key_value(head), swap(key_value(other))], axis=0)
        q_other = swap(columns(queries, other, group_columns))
        do_other = swap(columns(d_out, other, group_columns))
        shards = [own] + [ring(own, "ctx", s) for s in range(1, WIN)]
        blocks = group_columns // (HEADS * hd)
        flip_of = lambda n: n[1]
        first = attend(
            info, queries, d_out, shards, None, 2, lambda n: n[1], flip_of, (lambda n: n[1] * blocks, group_columns)
        )
        out, dq, total, *far = attend(
            info, q_other, do_other, shards, (first[2], first[0], first[1]), 2, lambda n: 1 - n[1], flip_of,
            (lambda n: 0, group_columns),
        )
    else:
        swap = lambda x: lax.all_to_all(x, "head", split_axis=1, concat_axis=0, tiled=True)
        own = jnp.concatenate([swap(keys), swap(values)], axis=1)
        shards = [own] + [ring(own, "ctx", s) for s in range(1, WIN)]
        zero = lambda n: 0
        out, dq, total, *far = attend(
            info, swap(queries), swap(d_out), shards, None, 1, zero, zero, (zero, group_columns)
        )
    near = [ring(x, "ctx", -s) for s, x in zip(range(1, WIN), far)]
    grad_keys, grad_values = pl.pallas_call(
        gather_kernel, out_shape=[jax.ShapeDtypeStruct((shard, hd), jnp.bfloat16)] * 2, name="gather"
    )(total, *near)
    return out, dq, grad_keys, grad_values


def solution(mesh):
    rows = P(("ctx", "head"), None)
    return jax.shard_map(
        body,
        mesh=mesh,
        in_specs=(rows, rows, rows, rows, P()),
        out_specs=(P("ctx", "head"),) * 4,
        check_vma=False,
    )
```

```python
import functools
import math

import jax
import jax.numpy as jnp
from jax import lax
from jax.experimental import pallas as pl
from jax.experimental.pallas import tpu as pltpu
from jax.sharding import PartitionSpec as P

WIN = 4
KEYS = 128
HEADS = 2
MASKED = -1e30
NT = (((1,), (1,)), ((), ()))
NN = (((1,), (0,)), ((), ()))
WHOLE = pl.BlockSpec(memory_space=pltpu.VMEM)
ANY = pl.BlockSpec(memory_space=pl.ANY)
SCALARS = pl.BlockSpec(memory_space=pltpu.SMEM)


def in_vmem(*arrays):
    return [pltpu.with_memory_space_constraint(x, pltpu.VMEM) for x in arrays]


def dot(a, b, dims):
    return lax.dot_general(a, b, dims, preferred_element_type=jnp.float32)


def fold(x, op):
    return op(x.reshape(x.shape[0] // 8, 8, x.shape[1]), axis=0)


def mask_kernel(lead, info, *bias_refs):
    keys, rows = bias_refs[0].shape
    shard = len(bias_refs) * rows
    for i, bias_ref in enumerate(bias_refs):
        tile = i ^ info[1] if len(bias_refs) > 1 else i
        first = info[0] * shard + tile * rows
        query = first + lax.broadcasted_iota(jnp.int32, (1, rows), 1)
        low = jnp.zeros((1, rows), jnp.int32)
        start = jnp.int32(0)
        for d in range(info.shape[0] - 2):
            low = jnp.where(query >= start, start, low)
            start = start + info[2 + d]
        for b in range(keys // KEYS):
            key = first - lead + b * KEYS + lax.broadcasted_iota(jnp.int32, (KEYS, rows), 0)
            ok = (key >= low) & (key <= query)
            bias_ref[b * KEYS : (b + 1) * KEYS, :] = jnp.where(ok, 0.0, MASKED)


def attend_kernel(tiles, index, info, q_hbm, do_hbm, bias_ref, *refs):
    shard_refs = refs[:WIN]
    refs = refs[WIN:]
    last = index == tiles - 1
    acc_in = None
    if index:
        acc_in = refs[0]
        refs = refs[3:]
    out_hbm, dq_hbm = refs[:2]
    if last:
        own_ref = refs[2]
        far_refs = refs[3 : 2 + WIN]
        refs = refs[2 + WIN :]
    else:
        acc_out = refs[2]
        refs = refs[3:]
    k_ref, v_ref, kt_ref, vt_ref, q_ref, do_ref, q_rows, do_rows, p_ref, ds_ref, out_ref, dq_ref, acc_ref, sem = refs

    shard, width = shard_refs[0].shape
    hd = width // 2
    keys, rows = bias_ref.shape
    lead = (WIN - 1) * shard
    blocks = keys // KEYS
    columns = out_hbm.shape[1]
    heads = columns // hd
    pairs = heads // HEADS
    flip = info[1] if tiles > 1 else 0
    tile = index ^ flip
    base = pl.multiple_of(tile * rows, KEYS)
    log2e = math.log2(math.e) / math.sqrt(hd)
    scaling = 1 / math.sqrt(hd)

    loads = []
    if q_hbm.shape[1] == columns:
        q_ref, do_ref = q_hbm, do_hbm
    else:
        mine = pl.ds(pl.multiple_of(info[1] * columns, 128), columns)
        loads = [
            pltpu.make_async_copy(q_hbm.at[:, mine], q_ref, sem.at[0]),
            pltpu.make_async_copy(do_hbm.at[:, mine], do_ref, sem.at[1]),
        ]
    for copy in loads:
        copy.start()
    part = shard // tiles
    for s in range(WIN):
        for j in range(tiles):
            at = pl.ds(pl.multiple_of((WIN - 1 - s) * shard + (j ^ flip) * part, KEYS), part)
            k_ref[at, :] = shard_refs[s][j * part : (j + 1) * part, :hd]
            v_ref[at, :] = shard_refs[s][j * part : (j + 1) * part, hd:]
    window = pl.ds(base, keys)
    for copy in loads:
        copy.wait()
    for h in range(heads):
        q_rows[h * rows : (h + 1) * rows, :] = q_ref[:, h * hd : (h + 1) * hd]
        do_rows[h * rows : (h + 1) * rows, :] = do_ref[:, h * hd : (h + 1) * hd]
    kt_ref[...] = k_ref[window, :].T
    vt_ref[...] = v_ref[window, :].T
    n = HEADS * rows

    def at(p):
        return slice(p * n, (p + 1) * n)

    def weights(p):
        s = dot(k_ref[window, :], q_rows[at(p), :], NT)
        s = s + jnp.concatenate([bias_ref[...]] * HEADS, axis=1)
        top = jnp.max(fold(s, jnp.max), axis=0, keepdims=True)
        e = jnp.exp2((s - top) * log2e)
        total = jnp.sum(fold(e, jnp.sum), axis=0, keepdims=True)
        p_f32 = e * (1.0 / total)
        p_ref[:, at(p)] = p_f32.astype(jnp.bfloat16)
        return p_f32

    def backward(p, p_f32):
        out = dot(vt_ref[...], p_ref[:, at(p)], NN).astype(jnp.bfloat16)
        do_t = do_rows[at(p), :].T.astype(jnp.float32)
        delta = jnp.sum(do_t * out.astype(jnp.float32), axis=0, keepdims=True)
        dp = dot(v_ref[window, :], do_rows[at(p), :], NT)
        ds_ref[:, at(p)] = (p_f32 * (dp - delta)).astype(jnp.bfloat16)
        dq = (dot(kt_ref[...], ds_ref[:, at(p)], NN) * scaling).astype(jnp.bfloat16)
        for i in range(HEADS):
            h = p * HEADS + i
            out_ref[:, h * hd : (h + 1) * hd] = out[:, i * rows : (i + 1) * rows].T
            dq_ref[:, h * hd : (h + 1) * hd] = dq[:, i * rows : (i + 1) * rows].T
        place = pl.ds(pl.multiple_of(tile * rows, rows), rows), pl.ds(p * HEADS * hd, HEADS * hd)
        here = slice(None), slice(p * HEADS * hd, (p + 1) * HEADS * hd)
        stores = [
            pltpu.make_async_copy(out_ref.at[here], out_hbm.at[place], sem.at[2 + 2 * p]),
            pltpu.make_async_copy(dq_ref.at[here], dq_hbm.at[place], sem.at[3 + 2 * p]),
        ]
        for copy in stores:
            copy.start()
        return stores

    stores = []
    ahead = weights(0)
    for p in range(pairs):
        now = ahead
        if p + 1 < pairs:
            ahead = weights(p + 1)
        stores += backward(p, now)
    dv = dot(p_ref[...], do_rows[...], NN)
    dk = dot(ds_ref[...], q_rows[...], NN)
    if not last:
        acc_out[...] = jnp.zeros_like(acc_out)
        acc_out[window, :hd] = dk
        acc_out[window, hd:] = dv
    else:
        if acc_in is None:
            acc_ref[:, :hd] = dk
            acc_ref[:, hd:] = dv
        else:
            acc_ref[...] = acc_in[...]
            acc_ref[window, :hd] += dk
            acc_ref[window, hd:] += dv
        own_ref[:, :hd] = acc_ref[lead:, :hd] * scaling
        own_ref[:, hd:] = acc_ref[lead:, hd:]
        for s in range(1, WIN):
            rows_of = slice((WIN - 1 - s) * shard, (WIN - s) * shard)
            far_refs[s - 1][:, :hd] = (acc_ref[rows_of, :hd] * scaling).astype(jnp.bfloat16)
            far_refs[s - 1][:, hd:] = acc_ref[rows_of, hd:].astype(jnp.bfloat16)
    for copy in stores:
        copy.wait()


def masks(info, shard, tiles):
    rows = shard // tiles
    lead = (WIN - 1) * shard
    return pl.pallas_call(
        functools.partial(mask_kernel, lead),
        out_shape=[pltpu.VMEM((lead + rows, rows), jnp.float32)] * tiles,
        in_specs=[SCALARS],
        out_specs=[WHOLE] * tiles,
        name="masks",
    )(info)


def attend(info, q, do, bias, shards, before, tiles, columns):
    shard, width = shards[0].shape
    hd = width // 2
    rows = shard // tiles
    index = 0 if before is None else 1
    last = index == tiles - 1
    keys = (WIN - 1) * shard + rows
    heads = columns // hd
    bf16, f32 = jnp.bfloat16, jnp.float32
    inner = q.shape[1] == columns
    args = [info, *(in_vmem(q, do) if inner else (q, do)), *in_vmem(bias, *shards)]
    in_specs = [SCALARS] + [WHOLE if inner else ANY] * 2 + [WHOLE] * (1 + WIN)
    aliases = {}
    if before is not None:
        aliases = {len(args) + 1: 0, len(args) + 2: 1}
        args += in_vmem(before[0]) + list(before[1:])
        in_specs += [WHOLE, ANY, ANY]
    out_shape = [jax.ShapeDtypeStruct((shard, columns), bf16)] * 2
    out_specs = [ANY, ANY]
    if last:
        out_shape += [pltpu.VMEM((shard, width), f32)] + [pltpu.VMEM((shard, width), bf16)] * (WIN - 1)
        out_specs += [WHOLE] * WIN
    else:
        out_shape += [pltpu.VMEM((WIN * shard, width), f32)]
        out_specs += [WHOLE]
    return pl.pallas_call(
        functools.partial(attend_kernel, tiles, index),
        out_shape=out_shape,
        in_specs=in_specs,
        out_specs=out_specs,
        scratch_shapes=[
            pltpu.VMEM((WIN * shard, hd), bf16),
            pltpu.VMEM((WIN * shard, hd), bf16),
            pltpu.VMEM((hd, keys), bf16),
            pltpu.VMEM((hd, keys), bf16),
            pltpu.VMEM((rows, columns) if not inner else (16, 128), bf16),
            pltpu.VMEM((rows, columns) if not inner else (16, 128), bf16),
            pltpu.VMEM((heads * rows, hd), bf16),
            pltpu.VMEM((heads * rows, hd), bf16),
            pltpu.VMEM((keys, heads * rows), bf16),
            pltpu.VMEM((keys, heads * rows), bf16),
            pltpu.VMEM((rows, columns), bf16),
            pltpu.VMEM((rows, columns), bf16),
            pltpu.VMEM((WIN * shard, width) if last else (8, 128), f32),
            pltpu.SemaphoreType.DMA((2 + 2 * (heads // HEADS),)),
        ],
        input_output_aliases=aliases,
        cost_estimate=pl.CostEstimate(
            flops=12 * keys * rows * columns, transcendentals=keys * rows * heads, bytes_accessed=1 << 21
        ),
        name="attend_last" if last else "attend_first",
    )(*args)


def gather_kernel(own_ref, *refs):
    total = own_ref[...]
    for r in refs[:-2]:
        total = total + r[...].astype(jnp.float32)
    hd = refs[-1].shape[1]
    refs[-2][...] = total[:, :hd].astype(jnp.bfloat16)
    refs[-1][...] = total[:, hd:].astype(jnp.bfloat16)


def ring(value, axis, steps):
    count = lax.axis_size(axis)
    return lax.ppermute(value, axis, [(i, (i + steps) % count) for i in range(count)])


def body(queries, keys, values, d_out, doc_lengths):
    count = lax.axis_size("head")
    head = lax.axis_index("head")
    part = queries.shape[0]
    shard = count * part
    hd = keys.shape[1] // count
    columns = queries.shape[1] // count
    info = jnp.concatenate([jnp.stack([lax.axis_index("ctx"), head]).astype(jnp.int32), doc_lengths])
    tiles = 2 if count == 2 else 1
    bias = masks(info, shard, tiles)
    if tiles == 2:
        other = 1 - head

        def half(x, index):
            width = x.shape[1] // 2
            return lax.dynamic_slice_in_dim(x, index * width, width, 1)

        def key_value(index):
            return jnp.concatenate([half(keys, index), half(values, index)], axis=1)

        def swap(x):
            return lax.ppermute(x, "head", [(0, 1), (1, 0)])

        own = jnp.concatenate([key_value(head), swap(key_value(other))], axis=0)
        q_other = swap(half(queries, other))
        do_other = swap(half(d_out, other))
        shards = [own] + [ring(own, "ctx", s) for s in range(1, WIN)]
        out, dq, acc = attend(info, queries, d_out, bias[0], shards, None, 2, columns)
        out, dq, total, *far = attend(info, q_other, do_other, bias[1], shards, (acc, out, dq), 2, columns)
    else:
        swap = lambda x: lax.all_to_all(x, "head", split_axis=1, concat_axis=0, tiled=True)
        own = jnp.concatenate([swap(keys), swap(values)], axis=1)
        shards = [own] + [ring(own, "ctx", s) for s in range(1, WIN)]
        out, dq, total, *far = attend(info, swap(queries), swap(d_out), bias[0], shards, None, 1, columns)
    near = [ring(x, "ctx", -s) for s, x in zip(range(1, WIN), far)]
    grad_keys, grad_values = pl.pallas_call(
        gather_kernel,
        out_shape=[jax.ShapeDtypeStruct((shard, hd), jnp.bfloat16)] * 2,
        in_specs=[WHOLE] * WIN,
        out_specs=[WHOLE] * 2,
        name="gather",
    )(*in_vmem(total, *near))
    return out, dq, grad_keys, grad_values


def solution(mesh):
    rows = P(("ctx", "head"), None)
    return jax.shard_map(
        body,
        mesh=mesh,
        in_specs=(rows, rows, rows, rows, P()),
        out_specs=(P("ctx", "head"),) * 4,
        check_vma=False,
    )
```

```python
import functools
import math

import jax
import jax.numpy as jnp
from jax import lax
from jax.experimental import pallas as pl
from jax.experimental.pallas import tpu as pltpu
from jax.sharding import PartitionSpec as P

WIN = 4
KEYS = 128
HEADS = 2
MASKED = -1e30
NT = (((1,), (1,)), ((), ()))
NN = (((1,), (0,)), ((), ()))
WHOLE = pl.BlockSpec(memory_space=pltpu.VMEM)
ANY = pl.BlockSpec(memory_space=pl.ANY)
SCALARS = pl.BlockSpec(memory_space=pltpu.SMEM)


def in_vmem(*arrays):
    return [pltpu.with_memory_space_constraint(x, pltpu.VMEM) for x in arrays]


def dot(a, b, dims):
    return lax.dot_general(a, b, dims, preferred_element_type=jnp.float32)


def fold(x, op):
    return op(x.reshape(x.shape[0] // 8, 8, x.shape[1]), axis=0)


def mask_kernel(lead, info, *bias_refs):
    keys, rows = bias_refs[0].shape
    shard = len(bias_refs) * rows
    for i, bias_ref in enumerate(bias_refs):
        tile = i ^ info[1] if len(bias_refs) > 1 else i
        first = info[0] * shard + tile * rows
        query = first + lax.broadcasted_iota(jnp.int32, (1, rows), 1)
        low = jnp.zeros((1, rows), jnp.int32)
        start = jnp.int32(0)
        for d in range(info.shape[0] - 2):
            low = jnp.where(query >= start, start, low)
            start = start + info[2 + d]
        for b in range(keys // KEYS):
            key = first - lead + b * KEYS + lax.broadcasted_iota(jnp.int32, (KEYS, rows), 0)
            ok = (key >= low) & (key <= query)
            bias_ref[b * KEYS : (b + 1) * KEYS, :] = jnp.where(ok, 0.0, MASKED)


def attend_kernel(tiles, index, info, q_hbm, do_hbm, bias_ref, *refs):
    shard_refs = refs[:WIN]
    refs = refs[WIN:]
    last = index == tiles - 1
    acc_in = None
    if index:
        acc_in = refs[0]
        refs = refs[3:]
    out_hbm, dq_hbm = refs[:2]
    if last:
        own_ref = refs[2]
        far_refs = refs[3 : 2 + WIN]
        refs = refs[2 + WIN :]
    else:
        acc_out = refs[2]
        refs = refs[3:]
    k_ref, v_ref, kt_ref, vt_ref, q_ref, do_ref, q_rows, do_rows, p_ref, ds_ref, out_ref, dq_ref, acc_ref, sem = refs

    shard, width = shard_refs[0].shape
    hd = width // 2
    keys, rows = bias_ref.shape
    lead = (WIN - 1) * shard
    blocks = keys // KEYS
    columns = out_hbm.shape[1]
    heads = columns // hd
    pairs = heads // HEADS
    flip = info[1] if tiles > 1 else 0
    tile = index ^ flip
    base = pl.multiple_of(tile * rows, KEYS)
    log2e = math.log2(math.e) / math.sqrt(hd)
    scaling = 1 / math.sqrt(hd)

    loads = []
    if q_hbm.shape[1] == columns:
        q_ref, do_ref = q_hbm, do_hbm
    else:
        mine = pl.ds(pl.multiple_of(info[1] * columns, 128), columns)
        loads = [
            pltpu.make_async_copy(q_hbm.at[:, mine], q_ref, sem.at[0]),
            pltpu.make_async_copy(do_hbm.at[:, mine], do_ref, sem.at[1]),
        ]
    for copy in loads:
        copy.start()
    part = shard // tiles
    for s in range(WIN):
        for j in range(tiles):
            at = pl.ds(pl.multiple_of((WIN - 1 - s) * shard + (j ^ flip) * part, KEYS), part)
            k_ref[at, :] = shard_refs[s][j * part : (j + 1) * part, :hd]
            v_ref[at, :] = shard_refs[s][j * part : (j + 1) * part, hd:]
    window = pl.ds(base, keys)
    for copy in loads:
        copy.wait()
    for h in range(heads):
        q_rows[h * rows : (h + 1) * rows, :] = q_ref[:, h * hd : (h + 1) * hd]
        do_rows[h * rows : (h + 1) * rows, :] = do_ref[:, h * hd : (h + 1) * hd]
    kt_ref[...] = k_ref[window, :].T
    vt_ref[...] = v_ref[window, :].T
    n = HEADS * rows

    def at(p):
        return slice(p * n, (p + 1) * n)

    def weights(p):
        s = dot(k_ref[window, :], q_rows[at(p), :], NT)
        s = s + jnp.concatenate([bias_ref[...]] * HEADS, axis=1)
        top = jnp.max(fold(s, jnp.max), axis=0, keepdims=True)
        e = jnp.exp2((s - top) * log2e)
        total = jnp.sum(fold(e, jnp.sum), axis=0, keepdims=True)
        p_f32 = e * (1.0 / total)
        p_ref[:, at(p)] = p_f32.astype(jnp.bfloat16)
        return p_f32

    def backward(p, p_f32):
        out = dot(vt_ref[...], p_ref[:, at(p)], NN).astype(jnp.bfloat16)
        do_t = do_rows[at(p), :].T.astype(jnp.float32)
        delta = jnp.sum(do_t * out.astype(jnp.float32), axis=0, keepdims=True)
        dp = dot(v_ref[window, :], do_rows[at(p), :], NT)
        ds_ref[:, at(p)] = (p_f32 * (dp - delta)).astype(jnp.bfloat16)
        dq = (dot(kt_ref[...], ds_ref[:, at(p)], NN) * scaling).astype(jnp.bfloat16)
        for i in range(HEADS):
            h = p * HEADS + i
            out_ref[:, h * hd : (h + 1) * hd] = out[:, i * rows : (i + 1) * rows].T
            dq_ref[:, h * hd : (h + 1) * hd] = dq[:, i * rows : (i + 1) * rows].T
        place = pl.ds(pl.multiple_of(tile * rows, rows), rows), pl.ds(p * HEADS * hd, HEADS * hd)
        here = slice(None), slice(p * HEADS * hd, (p + 1) * HEADS * hd)
        stores = [
            pltpu.make_async_copy(out_ref.at[here], out_hbm.at[place], sem.at[2 + 2 * p]),
            pltpu.make_async_copy(dq_ref.at[here], dq_hbm.at[place], sem.at[3 + 2 * p]),
        ]
        for copy in stores:
            copy.start()
        return stores

    stores = []
    ahead = weights(0)
    for p in range(pairs):
        now = ahead
        if p + 1 < pairs:
            ahead = weights(p + 1)
        stores += backward(p, now)
    dv = dot(p_ref[...], do_rows[...], NN)
    dk = dot(ds_ref[...], q_rows[...], NN)
    if not last:
        acc_out[...] = jnp.zeros_like(acc_out)
        acc_out[window, :hd] = dk
        acc_out[window, hd:] = dv
    else:
        if acc_in is None:
            acc_ref[:, :hd] = dk
            acc_ref[:, hd:] = dv
        else:
            acc_ref[...] = acc_in[...]
            acc_ref[window, :hd] += dk
            acc_ref[window, hd:] += dv
        own_ref[:, :hd] = acc_ref[lead:, :hd] * scaling
        own_ref[:, hd:] = acc_ref[lead:, hd:]
        for s in range(1, WIN):
            rows_of = slice((WIN - 1 - s) * shard, (WIN - s) * shard)
            far_refs[s - 1][:, :hd] = (acc_ref[rows_of, :hd] * scaling).astype(jnp.bfloat16)
            far_refs[s - 1][:, hd:] = acc_ref[rows_of, hd:].astype(jnp.bfloat16)
    for copy in stores:
        copy.wait()


def masks(info, shard, tiles):
    rows = shard // tiles
    lead = (WIN - 1) * shard
    return pl.pallas_call(
        functools.partial(mask_kernel, lead),
        out_shape=[pltpu.VMEM((lead + rows, rows), jnp.float32)] * tiles,
        in_specs=[SCALARS],
        out_specs=[WHOLE] * tiles,
        compiler_params=pltpu.CompilerParams(vmem_limit_bytes=4 << 20),
        name="masks",
    )(info)


def attend(info, q, do, bias, shards, before, tiles, columns):
    shard, width = shards[0].shape
    hd = width // 2
    rows = shard // tiles
    index = 0 if before is None else 1
    last = index == tiles - 1
    keys = (WIN - 1) * shard + rows
    heads = columns // hd
    bf16, f32 = jnp.bfloat16, jnp.float32
    inner = q.shape[1] == columns
    args = [info, *(in_vmem(q, do) if inner else (q, do)), *in_vmem(bias, *shards)]
    in_specs = [SCALARS] + [WHOLE if inner else ANY] * 2 + [WHOLE] * (1 + WIN)
    aliases = {}
    if before is not None:
        aliases = {len(args) + 1: 0, len(args) + 2: 1}
        args += in_vmem(before[0]) + list(before[1:])
        in_specs += [WHOLE, ANY, ANY]
    out_shape = [jax.ShapeDtypeStruct((shard, columns), bf16)] * 2
    out_specs = [ANY, ANY]
    if last:
        out_shape += [pltpu.VMEM((shard, width), f32)] + [pltpu.VMEM((shard, width), bf16)] * (WIN - 1)
        out_specs += [WHOLE] * WIN
    else:
        out_shape += [pltpu.VMEM((WIN * shard, width), f32)]
        out_specs += [WHOLE]
    return pl.pallas_call(
        functools.partial(attend_kernel, tiles, index),
        out_shape=out_shape,
        in_specs=in_specs,
        out_specs=out_specs,
        scratch_shapes=[
            pltpu.VMEM((WIN * shard, hd), bf16),
            pltpu.VMEM((WIN * shard, hd), bf16),
            pltpu.VMEM((hd, keys), bf16),
            pltpu.VMEM((hd, keys), bf16),
            pltpu.VMEM((rows, columns) if not inner else (16, 128), bf16),
            pltpu.VMEM((rows, columns) if not inner else (16, 128), bf16),
            pltpu.VMEM((heads * rows, hd), bf16),
            pltpu.VMEM((heads * rows, hd), bf16),
            pltpu.VMEM((keys, heads * rows), bf16),
            pltpu.VMEM((keys, heads * rows), bf16),
            pltpu.VMEM((rows, columns), bf16),
            pltpu.VMEM((rows, columns), bf16),
            pltpu.VMEM((WIN * shard, width) if last else (8, 128), f32),
            pltpu.SemaphoreType.DMA((2 + 2 * (heads // HEADS),)),
        ],
        input_output_aliases=aliases,
        compiler_params=pltpu.CompilerParams(vmem_limit_bytes=24 << 20),
        cost_estimate=pl.CostEstimate(
            flops=12 * keys * rows * columns, transcendentals=keys * rows * heads, bytes_accessed=1 << 21
        ),
        name="attend_last" if last else "attend_first",
    )(*args)


def gather_kernel(own_ref, *refs):
    total = own_ref[...]
    for r in refs[:-2]:
        total = total + r[...].astype(jnp.float32)
    hd = refs[-1].shape[1]
    refs[-2][...] = total[:, :hd].astype(jnp.bfloat16)
    refs[-1][...] = total[:, hd:].astype(jnp.bfloat16)


def ring(value, axis, steps):
    count = lax.axis_size(axis)
    return lax.ppermute(value, axis, [(i, (i + steps) % count) for i in range(count)])


def body(queries, keys, values, d_out, doc_lengths):
    count = lax.axis_size("head")
    head = lax.axis_index("head")
    part = queries.shape[0]
    shard = count * part
    hd = keys.shape[1] // count
    columns = queries.shape[1] // count
    info = jnp.concatenate([jnp.stack([lax.axis_index("ctx"), head]).astype(jnp.int32), doc_lengths])
    tiles = 2 if count == 2 else 1
    bias = masks(info, shard, tiles)
    if tiles == 2:
        other = 1 - head

        def half(x, index):
            width = x.shape[1] // 2
            return lax.dynamic_slice_in_dim(x, index * width, width, 1)

        def key_value(index):
            return jnp.concatenate([half(keys, index), half(values, index)], axis=1)

        def swap(x):
            return lax.ppermute(x, "head", [(0, 1), (1, 0)])

        own = jnp.concatenate([key_value(head), swap(key_value(other))], axis=0)
        q_other = swap(half(queries, other))
        do_other = swap(half(d_out, other))
        shards = [own] + [ring(own, "ctx", s) for s in range(1, WIN)]
        out, dq, acc = attend(info, queries, d_out, bias[0], shards, None, 2, columns)
        out, dq, total, *far = attend(info, q_other, do_other, bias[1], shards, (acc, out, dq), 2, columns)
    else:
        swap = lambda x: lax.all_to_all(x, "head", split_axis=1, concat_axis=0, tiled=True)
        own = jnp.concatenate([swap(keys), swap(values)], axis=1)
        shards = [own] + [ring(own, "ctx", s) for s in range(1, WIN)]
        out, dq, total, *far = attend(info, swap(queries), swap(d_out), bias[0], shards, None, 1, columns)
    near = [ring(x, "ctx", -s) for s, x in zip(range(1, WIN), far)]
    grad_keys, grad_values = pl.pallas_call(
        gather_kernel,
        out_shape=[jax.ShapeDtypeStruct((shard, hd), jnp.bfloat16)] * 2,
        in_specs=[WHOLE] * WIN,
        out_specs=[WHOLE] * 2,
        compiler_params=pltpu.CompilerParams(vmem_limit_bytes=4 << 20),
        name="gather",
    )(*in_vmem(total, *near))
    return out, dq, grad_keys, grad_values


def solution(mesh):
    rows = P(("ctx", "head"), None)
    return jax.shard_map(
        body,
        mesh=mesh,
        in_specs=(rows, rows, rows, rows, P()),
        out_specs=(P("ctx", "head"),) * 4,
        check_vma=False,
    )
```

```python
import functools
import math

import jax
import jax.numpy as jnp
from jax import lax
from jax.experimental import pallas as pl
from jax.experimental.pallas import tpu as pltpu
from jax.sharding import PartitionSpec as P

WIN = 4
KEYS = 128
HEADS = 2
MASKED = -1e30
NT = (((1,), (1,)), ((), ()))
NN = (((1,), (0,)), ((), ()))
WHOLE = pl.BlockSpec(memory_space=pltpu.VMEM)
ANY = pl.BlockSpec(memory_space=pl.ANY)
SCALARS = pl.BlockSpec(memory_space=pltpu.SMEM)


def in_vmem(*arrays):
    return [pltpu.with_memory_space_constraint(x, pltpu.VMEM) for x in arrays]


def dot(a, b, dims):
    return lax.dot_general(a, b, dims, preferred_element_type=jnp.float32)


def fold(x, op):
    return op(x.reshape(x.shape[0] // 8, 8, x.shape[1]), axis=0)


def mask_kernel(lead, info, *bias_refs):
    keys, rows = bias_refs[0].shape
    shard = len(bias_refs) * rows
    for i, bias_ref in enumerate(bias_refs):
        tile = i ^ info[1] if len(bias_refs) > 1 else i
        first = info[0] * shard + tile * rows
        query = first + lax.broadcasted_iota(jnp.int32, (1, rows), 1)
        low = jnp.zeros((1, rows), jnp.int32)
        start = jnp.int32(0)
        for d in range(info.shape[0] - 2):
            low = jnp.where(query >= start, start, low)
            start = start + info[2 + d]
        for b in range(keys // KEYS):
            key = first - lead + b * KEYS + lax.broadcasted_iota(jnp.int32, (KEYS, rows), 0)
            ok = (key >= low) & (key <= query)
            bias_ref[b * KEYS : (b + 1) * KEYS, :] = jnp.where(ok, 0.0, MASKED)


def attend_kernel(tiles, index, loaded, info, *refs):
    sources = refs[: 1 if loaded else 2]
    bias_ref = refs[len(sources)]
    refs = refs[len(sources) + 1 :]
    shard_refs = refs[:WIN]
    refs = refs[WIN:]
    last = index == tiles - 1
    acc_in = None
    if index:
        acc_in = refs[0]
        refs = refs[3:]
    out_hbm, dq_hbm = refs[:2]
    if last:
        own_ref = refs[2]
        far_refs = refs[3 : 2 + WIN]
        refs = refs[2 + WIN :]
    else:
        acc_out = refs[2]
        refs = refs[3:]
    k_ref, v_ref, kt_ref, vt_ref, q_do, q_rows, do_rows, p_ref, ds_ref, out_ref, dq_ref, acc_ref, sem = refs

    shard, width = shard_refs[0].shape
    hd = width // 2
    keys, rows = bias_ref.shape
    lead = (WIN - 1) * shard
    blocks = keys // KEYS
    columns = out_hbm.shape[1]
    heads = columns // hd
    pairs = heads // HEADS
    flip = info[1] if tiles > 1 else 0
    tile = index ^ flip
    base = pl.multiple_of(tile * rows, KEYS)
    log2e = math.log2(math.e) / math.sqrt(hd)
    scaling = 1 / math.sqrt(hd)

    loads = []
    if loaded:
        q_do = sources[0]
    else:
        mine = pl.ds(pl.multiple_of(info[1] * columns, 128), columns)
        for i, source in enumerate(sources):
            target = q_do.at[:, i * columns : (i + 1) * columns]
            loads.append(pltpu.make_async_copy(source.at[:, mine], target, sem.at[i]))
    for copy in loads:
        copy.start()
    part = shard // tiles
    odd = info[0] & 1
    starts = [(WIN - 1) * shard, odd * 2 * shard, shard, (1 - odd) * 2 * shard]
    for ref, start in zip(shard_refs, starts):
        for j in range(tiles):
            at = pl.ds(pl.multiple_of(start + (j ^ flip) * part, KEYS), part)
            k_ref[at, :] = ref[j * part : (j + 1) * part, :hd]
            v_ref[at, :] = ref[j * part : (j + 1) * part, hd:]
    window = pl.ds(base, keys)
    for copy in loads:
        copy.wait()
    for h in range(heads):
        q_rows[h * rows : (h + 1) * rows, :] = q_do[:, h * hd : (h + 1) * hd]
        do_rows[h * rows : (h + 1) * rows, :] = q_do[:, columns + h * hd : columns + (h + 1) * hd]
    kt_ref[...] = k_ref[window, :].T
    vt_ref[...] = v_ref[window, :].T
    n = HEADS * rows

    def at(p):
        return slice(p * n, (p + 1) * n)

    def weights(p):
        s = dot(k_ref[window, :], q_rows[at(p), :], NT)
        s = s + jnp.concatenate([bias_ref[...]] * HEADS, axis=1)
        top = jnp.max(fold(s, jnp.max), axis=0, keepdims=True)
        e = jnp.exp2((s - top) * log2e)
        total = jnp.sum(fold(e, jnp.sum), axis=0, keepdims=True)
        p_f32 = e * (1.0 / total)
        p_ref[:, at(p)] = p_f32.astype(jnp.bfloat16)
        return p_f32

    def backward(p, p_f32):
        out = dot(vt_ref[...], p_ref[:, at(p)], NN).astype(jnp.bfloat16)
        do_t = do_rows[at(p), :].T.astype(jnp.float32)
        delta = jnp.sum(do_t * out.astype(jnp.float32), axis=0, keepdims=True)
        dp = dot(v_ref[window, :], do_rows[at(p), :], NT)
        ds_ref[:, at(p)] = (p_f32 * (dp - delta)).astype(jnp.bfloat16)
        dq = (dot(kt_ref[...], ds_ref[:, at(p)], NN) * scaling).astype(jnp.bfloat16)
        for i in range(HEADS):
            h = p * HEADS + i
            out_ref[:, h * hd : (h + 1) * hd] = out[:, i * rows : (i + 1) * rows].T
            dq_ref[:, h * hd : (h + 1) * hd] = dq[:, i * rows : (i + 1) * rows].T
        place = pl.ds(pl.multiple_of(tile * rows, rows), rows), pl.ds(p * HEADS * hd, HEADS * hd)
        here = slice(None), slice(p * HEADS * hd, (p + 1) * HEADS * hd)
        stores = [
            pltpu.make_async_copy(out_ref.at[here], out_hbm.at[place], sem.at[2 + 2 * p]),
            pltpu.make_async_copy(dq_ref.at[here], dq_hbm.at[place], sem.at[3 + 2 * p]),
        ]
        for copy in stores:
            copy.start()
        return stores

    stores = []
    ahead = weights(0)
    for p in range(pairs):
        now = ahead
        if p + 1 < pairs:
            ahead = weights(p + 1)
        stores += backward(p, now)
    dv = dot(p_ref[...], do_rows[...], NN)
    dk = dot(ds_ref[...], q_rows[...], NN)
    if not last:
        acc_out[...] = jnp.zeros_like(acc_out)
        acc_out[window, :hd] = dk
        acc_out[window, hd:] = dv
    else:
        if acc_in is None:
            acc_ref[:, :hd] = dk
            acc_ref[:, hd:] = dv
        else:
            acc_ref[...] = acc_in[...]
            acc_ref[window, :hd] += dk
            acc_ref[window, hd:] += dv
        for ref, start in zip((own_ref, *far_refs), starts):
            rows_of = pl.ds(pl.multiple_of(start, KEYS), shard)
            ref[:, :hd] = (acc_ref[rows_of, :hd] * scaling).astype(ref.dtype)
            ref[:, hd:] = acc_ref[rows_of, hd:].astype(ref.dtype)
    for copy in stores:
        copy.wait()


def masks(info, shard, tiles):
    rows = shard // tiles
    lead = (WIN - 1) * shard
    return pl.pallas_call(
        functools.partial(mask_kernel, lead),
        out_shape=[pltpu.VMEM((lead + rows, rows), jnp.float32)] * tiles,
        in_specs=[SCALARS],
        out_specs=[WHOLE] * tiles,
        compiler_params=pltpu.CompilerParams(vmem_limit_bytes=4 << 20),
        name="masks",
    )(info)


def attend(info, q_do, bias, shards, before, tiles, columns):
    shard, width = shards[0].shape
    hd = width // 2
    rows = shard // tiles
    index = 0 if before is None else 1
    last = index == tiles - 1
    keys = (WIN - 1) * shard + rows
    heads = columns // hd
    bf16, f32 = jnp.bfloat16, jnp.float32
    inner = len(q_do) == 1
    args = [info, *(in_vmem(*q_do) if inner else q_do), *in_vmem(bias, *shards)]
    in_specs = [SCALARS] + [WHOLE if inner else ANY] * len(q_do) + [WHOLE] * (1 + WIN)
    aliases = {}
    if before is not None:
        aliases = {len(args) + 1: 0, len(args) + 2: 1}
        args += in_vmem(before[0]) + list(before[1:])
        in_specs += [WHOLE, ANY, ANY]
    out_shape = [jax.ShapeDtypeStruct((shard, columns), bf16)] * 2
    out_specs = [ANY, ANY]
    if last:
        out_shape += [pltpu.VMEM((shard, width), d) for d in (f32, bf16, f32, bf16)]
        out_specs += [WHOLE] * WIN
    else:
        out_shape += [pltpu.VMEM((WIN * shard, width), f32)]
        out_specs += [WHOLE]
    return pl.pallas_call(
        functools.partial(attend_kernel, tiles, index, inner),
        out_shape=out_shape,
        in_specs=in_specs,
        out_specs=out_specs,
        scratch_shapes=[
            pltpu.VMEM((WIN * shard, hd), bf16),
            pltpu.VMEM((WIN * shard, hd), bf16),
            pltpu.VMEM((hd, keys), bf16),
            pltpu.VMEM((hd, keys), bf16),
            pltpu.VMEM((16, 128) if inner else (rows, 2 * columns), bf16),
            pltpu.VMEM((heads * rows, hd), bf16),
            pltpu.VMEM((heads * rows, hd), bf16),
            pltpu.VMEM((keys, heads * rows), bf16),
            pltpu.VMEM((keys, heads * rows), bf16),
            pltpu.VMEM((rows, columns), bf16),
            pltpu.VMEM((rows, columns), bf16),
            pltpu.VMEM((WIN * shard, width) if last else (8, 128), f32),
            pltpu.SemaphoreType.DMA((2 + 2 * (heads // HEADS),)),
        ],
        input_output_aliases=aliases,
        compiler_params=pltpu.CompilerParams(vmem_limit_bytes=24 << 20),
        cost_estimate=pl.CostEstimate(
            flops=12 * keys * rows * columns, transcendentals=keys * rows * heads, bytes_accessed=1 << 21
        ),
        name="attend_last" if last else "attend_first",
    )(*args)


def gather_kernel(own_ref, *refs):
    total = own_ref[...]
    for r in refs[:-2]:
        total = total + r[...].astype(jnp.float32)
    hd = refs[-1].shape[1]
    refs[-2][...] = total[:, :hd].astype(jnp.bfloat16)
    refs[-1][...] = total[:, hd:].astype(jnp.bfloat16)


def move(value, kind, back=False):
    count = lax.axis_size("ctx")
    steps = {"A": lambda i: 3 if i % 2 else 1, "B": lambda i: 2, "C": lambda i: -1 if i % 2 else 1}[kind]
    pairs = [(i, (i + steps(i)) % count) for i in range(count)]
    return lax.ppermute(value, "ctx", [p[::-1] for p in pairs] if back else pairs)


def window(own):
    b = move(own, "B")
    a = move(own, "A")
    return [own, a, b, move(b, "C")]


def body(queries, keys, values, d_out, doc_lengths):
    count = lax.axis_size("head")
    head = lax.axis_index("head")
    part = queries.shape[0]
    shard = count * part
    hd = keys.shape[1] // count
    columns = queries.shape[1] // count
    info = jnp.concatenate([jnp.stack([lax.axis_index("ctx"), head]).astype(jnp.int32), doc_lengths])
    tiles = 2 if count == 2 else 1
    bias = masks(info, shard, tiles)
    if tiles == 2:
        other = 1 - head

        def half(x, index):
            width = x.shape[1] // 2
            return lax.dynamic_slice_in_dim(x, index * width, width, 1)

        def key_value(index):
            return jnp.concatenate([half(keys, index), half(values, index)], axis=1)

        def swap(x):
            return lax.ppermute(x, "head", [(0, 1), (1, 0)])

        own = jnp.concatenate([key_value(head), swap(key_value(other))], axis=0)
        both = swap(jnp.concatenate([half(queries, other), half(d_out, other)], axis=1))
        shards = window(own)
        out, dq, acc = attend(info, (queries, d_out), bias[0], shards, None, 2, columns)
        out, dq, total, *far = attend(info, (both,), bias[1], shards, (acc, out, dq), 2, columns)
    else:
        swap = lambda x: lax.all_to_all(x, "head", split_axis=1, concat_axis=0, tiled=True)
        own = jnp.concatenate([swap(keys), swap(values)], axis=1)
        shards = window(own)
        out, dq, total, *far = attend(
            info, (jnp.concatenate([swap(queries), swap(d_out)], axis=1),), bias[0], shards, None, 1, columns
        )
    far_c = move(far[2], "C", True)
    near_a = move(far[0], "A", True)
    near_b = move((far[1] + far_c.astype(jnp.float32)).astype(jnp.bfloat16), "B", True)
    grad_keys, grad_values = pl.pallas_call(
        gather_kernel,
        out_shape=[jax.ShapeDtypeStruct((shard, hd), jnp.bfloat16)] * 2,
        in_specs=[WHOLE] * 3,
        out_specs=[WHOLE] * 2,
        compiler_params=pltpu.CompilerParams(vmem_limit_bytes=4 << 20),
        name="gather",
    )(*in_vmem(total, near_a, near_b))
    return out, dq, grad_keys, grad_values


def solution(mesh):
    rows = P(("ctx", "head"), None)
    return jax.shard_map(
        body,
        mesh=mesh,
        in_specs=(rows, rows, rows, rows, P()),
        out_specs=(P("ctx", "head"),) * 4,
        check_vma=False,
    )
```

```python
import functools
import math

import jax
import jax.numpy as jnp
from jax import lax
from jax.experimental import pallas as pl
from jax.experimental.pallas import tpu as pltpu
from jax.sharding import PartitionSpec as P

WIN = 4
KEYS = 128
HEADS = 2
MASKED = -1e30
NT = (((1,), (1,)), ((), ()))
NN = (((1,), (0,)), ((), ()))
WHOLE = pl.BlockSpec(memory_space=pltpu.VMEM)
ANY = pl.BlockSpec(memory_space=pl.ANY)
SCALARS = pl.BlockSpec(memory_space=pltpu.SMEM)


def in_vmem(*arrays):
    return [pltpu.with_memory_space_constraint(x, pltpu.VMEM) for x in arrays]


def dot(a, b, dims):
    return lax.dot_general(a, b, dims, preferred_element_type=jnp.float32)


def fold(x, op):
    return op(x.reshape(x.shape[0] // 8, 8, x.shape[1]), axis=0)


def mask_kernel(lead, info, *bias_refs):
    keys, rows = bias_refs[0].shape
    shard = len(bias_refs) * rows
    for i, bias_ref in enumerate(bias_refs):
        tile = i ^ info[1] if len(bias_refs) > 1 else i
        first = info[0] * shard + tile * rows
        query = first + lax.broadcasted_iota(jnp.int32, (1, rows), 1)
        low = jnp.zeros((1, rows), jnp.int32)
        start = jnp.int32(0)
        for d in range(info.shape[0] - 2):
            low = jnp.where(query >= start, start, low)
            start = start + info[2 + d]
        for b in range(keys // KEYS):
            key = first - lead + b * KEYS + lax.broadcasted_iota(jnp.int32, (KEYS, rows), 0)
            ok = (key >= low) & (key <= query)
            bias_ref[b * KEYS : (b + 1) * KEYS, :] = jnp.where(ok, 0.0, MASKED)


def attend_kernel(tiles, index, loaded, info, *refs):
    sources = refs[: 1 if loaded else 2]
    bias_ref = refs[len(sources)]
    refs = refs[len(sources) + 1 :]
    shard_refs = refs[:WIN]
    refs = refs[WIN:]
    last = index == tiles - 1
    acc_refs = []
    if index:
        acc_refs = [refs[0]]
        refs = refs[3:]
    out_hbm, dq_hbm = refs[:2]
    if last:
        own_ref = refs[2]
        far_refs = refs[3 : 2 + WIN]
        refs = refs[2 + WIN :]
    else:
        refs = [*refs[3:-1], refs[2], refs[-1]]
    k_ref, v_ref, kt_ref, vt_ref, q_rows, do_rows, p_ref, ds_ref, out_ref, dq_ref, acc, sem = refs
    acc_refs.append(acc)

    shard, width = shard_refs[0].shape
    hd = width // 2
    keys, rows = bias_ref.shape
    lead = (WIN - 1) * shard
    blocks = keys // KEYS
    columns = out_hbm.shape[1]
    heads = columns // hd
    pairs = heads // HEADS
    flip = info[1] if tiles > 1 else 0
    tile = index ^ flip
    base = pl.multiple_of(tile * rows, KEYS)
    log2e = math.log2(math.e) / math.sqrt(hd)
    scaling = 1 / math.sqrt(hd)

    if loaded:
        q_do = [(sources[0], 0), (sources[0], columns)]
    else:
        mine = pl.multiple_of(info[1] * columns, 128)
        q_do = [(source, mine) for source in sources]
    part = shard // tiles
    odd = info[0] & 1
    starts = [(WIN - 1) * shard, odd * 2 * shard, shard, (1 - odd) * 2 * shard]
    for ref, start in zip(shard_refs, starts):
        for j in range(tiles):
            at = pl.ds(pl.multiple_of(start + (j ^ flip) * part, KEYS), part)
            k_ref[at, :] = ref[j * part : (j + 1) * part, :hd]
            v_ref[at, :] = ref[j * part : (j + 1) * part, hd:]
    window = pl.ds(base, keys)
    for (source, start), target in zip(q_do, (q_rows, do_rows)):
        for h in range(heads):
            target[h * rows : (h + 1) * rows, :] = source[:, pl.ds(start + h * hd, hd)]
    kt_ref[...] = k_ref[window, :].T
    vt_ref[...] = v_ref[window, :].T
    n = HEADS * rows

    def at(p):
        return slice(p * n, (p + 1) * n)

    def scores(p):
        s = dot(k_ref[window, :], q_rows[at(p), :], NT)
        s = s + jnp.concatenate([bias_ref[...]] * HEADS, axis=1)
        return s, jnp.max(fold(s, jnp.max), axis=0, keepdims=True)

    def weights(p, s, top):
        e = jnp.exp2((s - top) * log2e)
        total = jnp.sum(fold(e, jnp.sum), axis=0, keepdims=True)
        p_f32 = e * (1.0 / total)
        p_ref[:, at(p)] = p_f32.astype(jnp.bfloat16)
        return p_f32

    def columns_out(p, x, vmem, hbm, slot):
        for i in range(HEADS):
            h = p * HEADS + i
            vmem[:, h * hd : (h + 1) * hd] = x[:, i * rows : (i + 1) * rows].T
        here = slice(p * HEADS * hd, (p + 1) * HEADS * hd)
        place = pl.ds(pl.multiple_of(tile * rows, rows), rows)
        copy = pltpu.make_async_copy(vmem.at[:, here], hbm.at[place, here], sem.at[slot])
        copy.start()
        stores.append(copy)

    def outputs(p):
        out = dot(vt_ref[...], p_ref[:, at(p)], NN).astype(jnp.bfloat16)
        do_t = do_rows[at(p), :].T.astype(jnp.float32)
        delta = jnp.sum(do_t * out.astype(jnp.float32), axis=0, keepdims=True)
        columns_out(p, out, out_ref, out_hbm, 2 * p)
        return delta

    def dprobs(p):
        return dot(v_ref[window, :], do_rows[at(p), :], NT)

    def dscores(p, p_f32, dp, delta):
        ds_ref[:, at(p)] = (p_f32 * (dp - delta)).astype(jnp.bfloat16)

    def dqueries(p):
        dq = (dot(kt_ref[...], ds_ref[:, at(p)], NN) * scaling).astype(jnp.bfloat16)
        columns_out(p, dq, dq_ref, dq_hbm, 2 * p + 1)

    def sums(p):
        dk, dv = dot(ds_ref[:, at(p)], q_rows[at(p), :], NN), dot(p_ref[:, at(p)], do_rows[at(p), :], NN)
        if p:
            acc_ref[inside, :hd] += dk
            acc_ref[inside, hd:] += dv
        else:
            acc_ref[inside, :hd], acc_ref[inside, hd:] = dk, dv

    inside = slice(KEYS, KEYS + keys)
    acc_ref = acc_refs[-1]
    acc_ref[:KEYS, :] = jnp.zeros((KEYS, width), jnp.float32)
    acc_ref[KEYS + keys :, :] = jnp.zeros((KEYS, width), jnp.float32)
    stores = []
    w = weights(0, *scores(0))
    for p in range(pairs):
        nsc = scores(p + 1) if p + 1 < pairs else None
        dp = dprobs(p)
        delta = outputs(p)
        if p:
            dqueries(p - 1)
            sums(p - 1)
        nw = weights(p + 1, *nsc) if p + 1 < pairs else None
        dscores(p, w, dp, delta)
        w = nw
    dqueries(pairs - 1)
    sums(pairs - 1)
    if last:
        for ref, start in zip((own_ref, *far_refs), starts):
            total = None
            for i, acc in enumerate(acc_refs):
                at_tile = (i ^ flip) * rows if tiles > 1 else 0
                x = acc[pl.ds(pl.multiple_of(start - at_tile + KEYS, KEYS), shard), :]
                total = x if total is None else total + x
            ref[:, :hd] = (total[:, :hd] * scaling).astype(ref.dtype)
            ref[:, hd:] = total[:, hd:].astype(ref.dtype)
    for copy in stores:
        copy.wait()


def masks(info, shard, tiles):
    rows = shard // tiles
    lead = (WIN - 1) * shard
    return pl.pallas_call(
        functools.partial(mask_kernel, lead),
        out_shape=[pltpu.VMEM((lead + rows, rows), jnp.float32)] * tiles,
        in_specs=[SCALARS],
        out_specs=[WHOLE] * tiles,
        compiler_params=pltpu.CompilerParams(vmem_limit_bytes=4 << 20),
        name="masks",
    )(info)


def attend(info, q_do, bias, shards, before, tiles, columns):
    shard, width = shards[0].shape
    hd = width // 2
    rows = shard // tiles
    index = 0 if before is None else 1
    last = index == tiles - 1
    keys = (WIN - 1) * shard + rows
    heads = columns // hd
    bf16, f32 = jnp.bfloat16, jnp.float32
    acc = pltpu.VMEM((keys + 2 * KEYS, width), f32)
    inner = len(q_do) == 1
    args = [info, *in_vmem(*q_do, bias, *shards)]
    in_specs = [SCALARS] + [WHOLE] * (len(q_do) + 1 + WIN)
    aliases = {}
    if before is not None:
        aliases = {len(args) + 1: 0, len(args) + 2: 1}
        args += in_vmem(before[0]) + list(before[1:])
        in_specs += [WHOLE, ANY, ANY]
    out_shape = [jax.ShapeDtypeStruct((shard, columns), bf16)] * 2
    out_specs = [ANY, ANY]
    if last:
        out_shape += [pltpu.VMEM((shard, width), d) for d in (f32, bf16, f32, bf16)]
        out_specs += [WHOLE] * WIN
    else:
        out_shape += [acc]
        out_specs += [WHOLE]
    return pl.pallas_call(
        functools.partial(attend_kernel, tiles, index, inner),
        out_shape=out_shape,
        in_specs=in_specs,
        out_specs=out_specs,
        scratch_shapes=[
            pltpu.VMEM((WIN * shard, hd), bf16),
            pltpu.VMEM((WIN * shard, hd), bf16),
            pltpu.VMEM((hd, keys), bf16),
            pltpu.VMEM((hd, keys), bf16),
            pltpu.VMEM((heads * rows, hd), bf16),
            pltpu.VMEM((heads * rows, hd), bf16),
            pltpu.VMEM((keys, heads * rows), bf16),
            pltpu.VMEM((keys, heads * rows), bf16),
            pltpu.VMEM((rows, columns), bf16),
            pltpu.VMEM((rows, columns), bf16),
            *([acc] if last else []),
            pltpu.SemaphoreType.DMA((2 * (heads // HEADS),)),
        ],
        input_output_aliases=aliases,
        compiler_params=pltpu.CompilerParams(vmem_limit_bytes=24 << 20),
        cost_estimate=pl.CostEstimate(
            flops=12 * keys * rows * columns, transcendentals=keys * rows * heads, bytes_accessed=1 << 21
        ),
        name="attend_last" if last else "attend_first",
    )(*args)


def gather_kernel(own_ref, *refs):
    total = own_ref[...]
    for r in refs[:-2]:
        total = total + r[...].astype(jnp.float32)
    hd = refs[-1].shape[1]
    refs[-2][...] = total[:, :hd].astype(jnp.bfloat16)
    refs[-1][...] = total[:, hd:].astype(jnp.bfloat16)


def move(value, kind, back=False):
    count = lax.axis_size("ctx")
    steps = {"A": lambda i: 3 if i % 2 else 1, "B": lambda i: 2, "C": lambda i: -1 if i % 2 else 1}[kind]
    pairs = [(i, (i + steps(i)) % count) for i in range(count)]
    return lax.ppermute(value, "ctx", [p[::-1] for p in pairs] if back else pairs)


def window(own, bias):
    b = move(own, "B")
    a = move(own, "A")
    b, *bias = lax.optimization_barrier((b, *bias))
    return [own, a, b, move(b, "C")], bias


def body(queries, keys, values, d_out, doc_lengths):
    count = lax.axis_size("head")
    head = lax.axis_index("head")
    part = queries.shape[0]
    shard = count * part
    hd = keys.shape[1] // count
    columns = queries.shape[1] // count
    info = jnp.concatenate([jnp.stack([lax.axis_index("ctx"), head]).astype(jnp.int32), doc_lengths])
    tiles = 2 if count == 2 else 1
    bias = masks(info, shard, tiles)
    if tiles == 2:
        other = 1 - head

        def half(x, index):
            width = x.shape[1] // 2
            return lax.dynamic_slice_in_dim(x, index * width, width, 1)

        def key_value(index):
            return jnp.concatenate([half(keys, index), half(values, index)], axis=1)

        def swap(x):
            return lax.ppermute(x, "head", [(0, 1), (1, 0)])

        own = jnp.concatenate([key_value(head), swap(key_value(other))], axis=0)
        both = swap(jnp.concatenate([half(queries, other), half(d_out, other)], axis=1))
        shards, bias = window(own, bias)
        out, dq, acc = attend(info, (queries, d_out), bias[0], shards, None, 2, columns)
        out, dq, total, *far = attend(info, (both,), bias[1], shards, (acc, out, dq), 2, columns)
    else:
        swap = lambda x: lax.all_to_all(x, "head", split_axis=1, concat_axis=0, tiled=True)
        own = jnp.concatenate([swap(keys), swap(values)], axis=1)
        shards, bias = window(own, bias)
        out, dq, total, *far = attend(
            info, (jnp.concatenate([swap(queries), swap(d_out)], axis=1),), bias[0], shards, None, 1, columns
        )
    far_c = move(far[2], "C", True)
    near_a = move(far[0], "A", True)
    near_b = move((far[1] + far_c.astype(jnp.float32)).astype(jnp.bfloat16), "B", True)
    grad_keys, grad_values = pl.pallas_call(
        gather_kernel,
        out_shape=[jax.ShapeDtypeStruct((shard, hd), jnp.bfloat16)] * 2,
        in_specs=[WHOLE] * 3,
        out_specs=[WHOLE] * 2,
        compiler_params=pltpu.CompilerParams(vmem_limit_bytes=4 << 20),
        name="gather",
    )(*in_vmem(total, near_a, near_b))
    return out, dq, grad_keys, grad_values


def solution(mesh):
    rows = P(("ctx", "head"), None)
    return jax.shard_map(
        body,
        mesh=mesh,
        in_specs=(rows, rows, rows, rows, P()),
        out_specs=(P("ctx", "head"),) * 4,
        check_vma=False,
    )
```

```python
import functools
import math

import jax
import jax.numpy as jnp
from jax import lax
from jax.experimental import pallas as pl
from jax.experimental.pallas import tpu as pltpu
from jax.sharding import PartitionSpec as P

WIN = 4
HEADS = 2
MASKED = -1e30
NT = (((1,), (1,)), ((), ()))
NN = (((1,), (0,)), ((), ()))
WHOLE = pl.BlockSpec(memory_space=pltpu.VMEM)
ANY = pl.BlockSpec(memory_space=pl.ANY)
SCALARS = pl.BlockSpec(memory_space=pltpu.SMEM)
BF16, F32 = jnp.bfloat16, jnp.float32

OWN, A, B, C = range(WIN)
SLOTS = {1: ((OWN, 0), (B, 0), (A, 0), (C, 0)), 2: ((OWN, None), (B, 1), (B, 0), (A, 1), (A, 0), (C, 1), (C, 0))}
EARLY = 5


def in_vmem(*arrays):
    return [pltpu.with_memory_space_constraint(x, pltpu.VMEM) for x in arrays]


def dot(a, b, dims):
    return lax.dot_general(a, b, dims, preferred_element_type=F32)


def fold(x, op):
    return op(x.reshape(x.shape[0] // 8, 8, x.shape[1]), axis=0)


def distances(info):
    odd = info[0] & 1
    return {OWN: 0, A: 3 - 2 * odd, B: 2, C: 1 + 2 * odd}


def moved(info, tile, shard):
    if shard not in (A, C):
        return None
    odd = info[0] & 1
    return (tile == 1) & (odd == (1 if shard == C else 0))


def tile_of(info, tiles, index):
    return index ^ info[1] if tiles == 2 else index


def stored(info, tiles, part):
    return part ^ info[1] if tiles == 2 else part


def mask_kernel(shard, info, *bias_refs):
    tiles = len(bias_refs)
    part = shard // tiles
    back = distances(info)
    for index, bias_ref in enumerate(bias_refs):
        tile = tile_of(info, tiles, index)
        first = info[0] * shard + tile * part
        query = first + lax.broadcasted_iota(jnp.int32, (1, part), 1)
        low = jnp.zeros((1, part), jnp.int32)
        start = jnp.int32(0)
        for d in range(info.shape[0] - 2):
            low = jnp.where(query >= start, start, low)
            start = start + info[2 + d]
        for slot, (s, j) in enumerate(SLOTS[tiles]):
            at = (info[0] - back[s]) * shard + (tile if j is None else j) * part
            if tiles == 2 and j == 0 and moved(info, tile, s) is not None:
                at = jnp.where(moved(info, tile, s), info[0] * shard, at)
            key = at + lax.broadcasted_iota(jnp.int32, (part, part), 0)
            ok = (key >= low) & (key <= query)
            bias_ref[slot * part : (slot + 1) * part, :] = jnp.where(ok, 0.0, MASKED)


def fill(info, tiles, tile, shard_refs, slots, k_ref=None, v_ref=None):
    shard, width = shard_refs[0].shape
    part, hd = shard // tiles, width // 2

    def rows(s, j):
        return shard_refs[s][pl.ds(pl.multiple_of(stored(info, tiles, j) * part, part), part), :]

    for slot in slots:
        s, j = SLOTS[tiles][slot]
        x = rows(s, tile if j is None else j)
        if tiles == 2 and j == 0 and moved(info, tile, s) is not None:
            x = jnp.where(moved(info, tile, s), rows(OWN, 0), x)
        at = slice(slot * part, (slot + 1) * part)
        if k_ref is not None:
            k_ref[at, :] = x[:, :hd]
        if v_ref is not None:
            v_ref[at, :] = x[:, hd:]


def by_heads(info, sources, columns, rows, hd, *targets):
    if len(sources) == 1:
        places = [(sources[0], 0), (sources[0], columns)]
    else:
        mine = pl.multiple_of(info[1] * columns, 128)
        places = [(source, mine) for source in sources]
    for (source, start), target in zip(places, targets):
        for h in range(columns // hd):
            target[h * rows : (h + 1) * rows, :] = source[:, pl.ds(start + h * hd, hd)]


def scores_of(k, q, bias):
    s = dot(k, q, NT) + jnp.concatenate([bias] * HEADS, axis=1)
    return s, jnp.max(fold(s, jnp.max), axis=0, keepdims=True)


def early_kernel(info, q_ref, do_ref, bias_ref, *refs):
    shard_refs, (e_ref, dp_ref, top_ref, sum_ref, k_ref, v_ref, q_rows, do_rows) = refs[:3], refs[3:]
    rows = bias_ref.shape[1]
    hd = k_ref.shape[1]
    early = e_ref.shape[0]
    n = HEADS * rows
    log2e = math.log2(math.e) / math.sqrt(hd)
    fill(info, 2, tile_of(info, 2, 0), shard_refs, range(EARLY), k_ref, v_ref)
    by_heads(info, (q_ref, do_ref), q_ref.shape[1] // 2, rows, hd, q_rows, do_rows)
    pairs = q_rows.shape[0] // n
    sc = scores_of(k_ref[...], q_rows[:n, :], bias_ref[:early, :])
    for p in range(pairs):
        at = slice(p * n, (p + 1) * n)
        s, top = sc
        if p + 1 < pairs:
            sc = scores_of(k_ref[...], q_rows[(p + 1) * n : (p + 2) * n, :], bias_ref[:early, :])
        dp_ref[:, at] = dot(v_ref[...], do_rows[at, :], NT)
        e = jnp.exp2((s - top) * log2e)
        e_ref[:, at] = e
        top_ref[:, at] = top
        sum_ref[:, at] = jnp.sum(fold(e, jnp.sum), axis=0, keepdims=True)


def attend_kernel(tiles, index, info, *refs):
    last = index == tiles - 1
    ahead = not last
    sources, refs = (refs[:2], refs[2:]) if ahead else (refs[:1], refs[1:])
    bias_ref, *refs = refs
    shard_refs, refs = refs[:WIN], refs[WIN:]
    acc_refs = []
    if ahead:
        (e_early, dp_early, top_early, sum_early), refs = refs[:4], refs[4:]
    if index:
        acc_refs, refs = [refs[0]], refs[2:]
    out_hbm, ds_ref, *refs = refs
    if last:
        grad_refs, refs = refs[:WIN], refs[WIN:]
        acc_refs.append(refs[0])
    else:
        acc_refs.append(refs[0])
    acc_ref, k_ref, v_ref, vt_ref, q_rows, do_rows, p_ref, out_ref, sem = refs

    shard, width = shard_refs[0].shape
    hd = width // 2
    keys, rows = bias_ref.shape
    columns = out_hbm.shape[1]
    pairs = columns // hd // HEADS
    part = shard // tiles
    tile = tile_of(info, tiles, index)
    n = HEADS * rows
    early = EARLY * part if ahead else 0
    log2e = math.log2(math.e) / math.sqrt(hd)
    scaling = 1 / math.sqrt(hd)
    fill(info, tiles, tile, shard_refs, range(len(SLOTS[tiles])), k_ref, v_ref)
    by_heads(info, sources, columns, rows, hd, q_rows, do_rows)
    vt_ref[...] = v_ref[...].T

    def at(p):
        return slice(p * n, (p + 1) * n)

    def scores(p):
        return scores_of(k_ref[early:, :], q_rows[at(p), :], bias_ref[early:, :])

    def weights(p, s, top):
        if ahead:
            before = top_early[:, at(p)]
            top = jnp.maximum(top, before)
            rescale = jnp.exp2((before - top) * log2e)
        e = jnp.exp2((s - top) * log2e)
        total = jnp.sum(fold(e, jnp.sum), axis=0, keepdims=True)
        if ahead:
            total = total + sum_early[:, at(p)] * rescale
        inverse = 1.0 / total
        p_f32 = e * inverse
        p_ref[early:, at(p)] = p_f32.astype(BF16)
        if ahead:
            first = e_early[:, at(p)] * (rescale * inverse)
            p_ref[:early, at(p)] = first.astype(BF16)
            return first, p_f32
        return (p_f32,)

    def outputs(p):
        out = dot(vt_ref[...], p_ref[:, at(p)], NN).astype(BF16)
        do_t = do_rows[at(p), :].T.astype(F32)
        delta = jnp.sum(do_t * out.astype(F32), axis=0, keepdims=True)
        for i in range(HEADS):
            h = p * HEADS + i
            out_ref[:, h * hd : (h + 1) * hd] = out[:, i * rows : (i + 1) * rows].T
        here = slice(p * HEADS * hd, (p + 1) * HEADS * hd)
        place = pl.ds(pl.multiple_of(tile * rows, rows), rows)
        copy = pltpu.make_async_copy(out_ref.at[:, here], out_hbm.at[place, here], sem.at[p])
        copy.start()
        stores.append(copy)
        return delta

    def dprobs(p):
        return dot(v_ref[early:, :], do_rows[at(p), :], NT)

    def dscores(p, w, dp, delta):
        if ahead:
            ds_ref[:early, at(p)] = (w[0] * (dp_early[:, at(p)] - delta)).astype(BF16)
        ds_ref[early:, at(p)] = (w[-1] * (dp - delta)).astype(BF16)

    def sums(p):
        dk, dv = dot(ds_ref[:, at(p)], q_rows[at(p), :], NN), dot(p_ref[:, at(p)], do_rows[at(p), :], NN)
        if p:
            acc_ref[:, :hd] += dk
            acc_ref[:, hd:] += dv
        else:
            acc_ref[:, :hd], acc_ref[:, hd:] = dk, dv

    stores = []
    w = weights(0, *scores(0))
    for p in range(pairs):
        following = scores(p + 1) if p + 1 < pairs else None
        dp = dprobs(p)
        delta = outputs(p)
        if p:
            sums(p - 1)
        nw = weights(p + 1, *following) if p + 1 < pairs else None
        dscores(p, w, dp, delta)
        w = nw
    sums(pairs - 1)
    if last:

        def give(ref, row, x):
            where = pl.ds(pl.multiple_of(row * part, part), part)
            ref[where, :hd] = (x[:, :hd] * scaling).astype(ref.dtype)
            ref[where, hd:] = x[:, hd:].astype(ref.dtype)

        parts = [[acc[slot * part : (slot + 1) * part, :] for acc in acc_refs] for slot in range(len(SLOTS[tiles]))]
        own = list(parts[0])
        for (s, j), xs in list(zip(SLOTS[tiles], parts))[1:]:
            if tiles == 2 and j == 0 and s in (A, C):
                for i, x in enumerate(xs):
                    keep = jnp.where(moved(info, tile_of(info, tiles, i), s), 0.0, 1.0)
                    own[1 - i] = own[1 - i] + x * (1.0 - keep)
                    xs[i] = x * keep
            give(grad_refs[s], stored(info, tiles, j), sum(xs[1:], xs[0]))
        for i, x in enumerate(own):
            give(grad_refs[OWN], i, x)
    for copy in stores:
        copy.wait()


def queries_kernel(tiles, info, *refs):
    shard_refs, refs = refs[:WIN], refs[WIN:]
    ds_refs, (dq_hbm, k_ref, kt_ref, dq_ref, sem) = refs[:tiles], refs[tiles:]
    hd, keys = kt_ref.shape
    rows = dq_hbm.shape[0] // tiles
    n = HEADS * rows
    width = HEADS * hd
    stores = []
    for index, ds_ref in enumerate(ds_refs):
        tile = tile_of(info, tiles, index)
        fill(info, tiles, tile, shard_refs, range(len(SLOTS[tiles])), k_ref)
        kt_ref[...] = k_ref[...].T
        for p in range(ds_ref.shape[1] // n):
            dq = (dot(kt_ref[...], ds_ref[:, p * n : (p + 1) * n], NN) * (1 / math.sqrt(hd))).astype(BF16)
            for i in range(HEADS):
                here = slice(p * width + i * hd, p * width + (i + 1) * hd)
                dq_ref[index * rows : (index + 1) * rows, here] = dq[:, i * rows : (i + 1) * rows].T
            here = slice(p * width, (p + 1) * width)
            place = pl.ds(pl.multiple_of(tile * rows, rows), rows)
            source = dq_ref.at[index * rows : (index + 1) * rows, here]
            copy = pltpu.make_async_copy(source, dq_hbm.at[place, here], sem.at[len(stores)])
            copy.start()
            stores.append(copy)
    for copy in stores:
        copy.wait()


def params(mib):
    return pltpu.CompilerParams(vmem_limit_bytes=mib << 20)


def masks(info, shard, tiles):
    part = shard // tiles
    return pl.pallas_call(
        functools.partial(mask_kernel, shard),
        out_shape=[pltpu.VMEM((len(SLOTS[tiles]) * part, part), F32)] * tiles,
        in_specs=[SCALARS],
        out_specs=[WHOLE] * tiles,
        compiler_params=params(4),
        name="masks",
    )(info)


def early(info, queries, d_out, bias, shards, columns):
    shard, width = shards[0].shape
    part, hd = shard // 2, width // 2
    all_rows = columns // hd * part
    keys = EARLY * part
    row = pltpu.VMEM((1, all_rows), F32)
    return pl.pallas_call(
        early_kernel,
        out_shape=[pltpu.VMEM((keys, all_rows), F32)] * 2 + [row, row],
        in_specs=[SCALARS] + [WHOLE] * 6,
        out_specs=[WHOLE] * 4,
        scratch_shapes=[pltpu.VMEM((keys, hd), BF16)] * 2 + [pltpu.VMEM((all_rows, hd), BF16)] * 2,
        compiler_params=params(16),
        cost_estimate=pl.CostEstimate(
            flops=4 * keys * all_rows * hd, transcendentals=keys * all_rows, bytes_accessed=1 << 21
        ),
        name="early",
    )(info, *in_vmem(queries, d_out, bias, *shards))


def attend(info, q_do, bias, shards, prepared, before, tiles, columns):
    shard, width = shards[0].shape
    hd = width // 2
    index = 0 if before is None else 1
    last = index == tiles - 1
    keys, rows = bias.shape
    all_rows = columns // hd * rows
    acc = pltpu.VMEM((keys, width), F32)
    args = [info, *in_vmem(*q_do, bias, *shards, *prepared)]
    in_specs = [SCALARS] + [WHOLE] * (len(args) - 1)
    aliases = {}
    if before is not None:
        aliases = {len(args) + 1: 0}
        args += [*in_vmem(before[0]), before[1]]
        in_specs += [WHOLE, ANY]
    out_shape = [jax.ShapeDtypeStruct((shard, columns), BF16), pltpu.VMEM((keys, all_rows), BF16)]
    if last:
        out_shape += [pltpu.VMEM((shard, width), d) for d in (F32, BF16, F32, BF16)]
    else:
        out_shape += [acc]
    return pl.pallas_call(
        functools.partial(attend_kernel, tiles, index),
        out_shape=out_shape,
        in_specs=in_specs,
        out_specs=[ANY] + [WHOLE] * (len(out_shape) - 1),
        scratch_shapes=[
            *([acc] if last else []),
            pltpu.VMEM((keys, hd), BF16),
            pltpu.VMEM((keys, hd), BF16),
            pltpu.VMEM((hd, keys), BF16),
            pltpu.VMEM((all_rows, hd), BF16),
            pltpu.VMEM((all_rows, hd), BF16),
            pltpu.VMEM((keys, all_rows), BF16),
            pltpu.VMEM((rows, columns), BF16),
            pltpu.SemaphoreType.DMA((columns // hd // HEADS,)),
        ],
        input_output_aliases=aliases,
        compiler_params=params(24),
        cost_estimate=pl.CostEstimate(
            flops=10 * keys * rows * columns, transcendentals=keys * all_rows, bytes_accessed=1 << 21
        ),
        name="attend_last" if last else "attend_first",
    )(*args)


def query_gradients(info, shards, dscores, columns):
    shard, width = shards[0].shape
    tiles = len(dscores)
    hd, keys = width // 2, dscores[0].shape[0]
    return pl.pallas_call(
        functools.partial(queries_kernel, tiles),
        out_shape=jax.ShapeDtypeStruct((shard, columns), BF16),
        in_specs=[SCALARS] + [WHOLE] * (WIN + tiles),
        out_specs=ANY,
        scratch_shapes=[
            pltpu.VMEM((keys, hd), BF16),
            pltpu.VMEM((hd, keys), BF16),
            pltpu.VMEM((shard, columns), BF16),
            pltpu.SemaphoreType.DMA((tiles * (columns // hd // HEADS),)),
        ],
        compiler_params=params(12),
        cost_estimate=pl.CostEstimate(flops=2 * keys * shard * columns, transcendentals=0, bytes_accessed=1 << 21),
        name="query_gradients",
    )(info, *in_vmem(*shards, *dscores))


def gather_kernel(own_ref, *refs):
    total = own_ref[...]
    for r in refs[:-2]:
        total = total + r[...].astype(F32)
    hd = refs[-1].shape[1]
    refs[-2][...] = total[:, :hd].astype(BF16)
    refs[-1][...] = total[:, hd:].astype(BF16)


def in_order_kernel(info, own_ref, *refs):
    near, (k_ref, v_ref) = refs[:-2], refs[-2:]
    shard, hd = k_ref.shape
    part = shard // 2
    total = own_ref[...]
    for r in near:
        total = total + r[...].astype(F32)
    for j in range(2):
        to = pl.ds(pl.multiple_of((j ^ info[1]) * part, part), part)
        k_ref[to, :] = total[j * part : (j + 1) * part, :hd].astype(BF16)
        v_ref[to, :] = total[j * part : (j + 1) * part, hd:].astype(BF16)


def move(value, kind, back=False):
    count = lax.axis_size("ctx")
    steps = {A: lambda i: 3 if i % 2 else 1, B: lambda i: 2, C: lambda i: -1 if i % 2 else 1}[kind]
    pairs = [(i, (i + steps(i)) % count) for i in range(count)]
    return lax.ppermute(value, "ctx", [p[::-1] for p in pairs] if back else pairs)


def window(own, bias):
    b = move(own, B)
    a = move(own, A)
    b, *bias = lax.optimization_barrier((b, *bias))
    return [own, a, b, move(b, C)], bias


def body(queries, keys, values, d_out, doc_lengths):
    count = lax.axis_size("head")
    head = lax.axis_index("head")
    shard = count * queries.shape[0]
    hd = keys.shape[1] // count
    columns = queries.shape[1] // count
    info = jnp.concatenate([jnp.stack([lax.axis_index("ctx"), head]).astype(jnp.int32), doc_lengths])
    tiles = 2 if count == 2 else 1
    bias = masks(info, shard, tiles)
    if tiles == 2:
        other = 1 - head

        def half(x, index):
            width = x.shape[1] // 2
            return lax.dynamic_slice_in_dim(x, index * width, width, 1)

        def key_value(index):
            return jnp.concatenate([half(keys, index), half(values, index)], axis=1)

        def swap(x):
            return lax.ppermute(x, "head", [(0, 1), (1, 0)])

        own = jnp.concatenate([key_value(head), swap(key_value(other))], axis=0)
        both = swap(jnp.concatenate([half(queries, other), half(d_out, other)], axis=1))
        shards, bias = window(own, bias)
        prepared = early(info, queries, d_out, bias[0], shards[:C], columns)
        out, ds_first, acc = attend(info, (queries, d_out), bias[0], shards, prepared, None, 2, columns)
        out, ds_last, *grads = attend(info, (both,), bias[1], shards, (), (acc, out), 2, columns)
        dscores = (ds_first, ds_last)
    else:
        swap = lambda x: lax.all_to_all(x, "head", split_axis=1, concat_axis=0, tiled=True)
        own = jnp.concatenate([swap(keys), swap(values)], axis=1)
        both = jnp.concatenate([swap(queries), swap(d_out)], axis=1)
        shards, bias = window(own, bias)
        out, ds_last, *grads = attend(info, (both,), bias[0], shards, (), None, 1, columns)
        dscores = (ds_last,)
    from_c = move(grads[C], C, True)
    near_a = move(grads[A], A, True)
    near_b = move((grads[B] + from_c.astype(F32)).astype(BF16), B, True)
    dq = query_gradients(info, shards, dscores, columns)
    ordered = [info] if tiles == 2 else []
    grad_keys, grad_values = pl.pallas_call(
        in_order_kernel if tiles == 2 else gather_kernel,
        out_shape=[jax.ShapeDtypeStruct((shard, hd), BF16)] * 2,
        in_specs=[SCALARS] * len(ordered) + [WHOLE] * 3,
        out_specs=[WHOLE] * 2,
        compiler_params=params(4),
        name="gather",
    )(*ordered, *in_vmem(grads[OWN], near_a, near_b))
    return out, dq, grad_keys, grad_values


def solution(mesh):
    rows = P(("ctx", "head"), None)
    return jax.shard_map(
        body,
        mesh=mesh,
        in_specs=(rows, rows, rows, rows, P()),
        out_specs=(P("ctx", "head"),) * 4,
        check_vma=False,
    )
```

```python
import functools
import math

import jax
import jax.numpy as jnp
from jax import lax
from jax.experimental import pallas as pl
from jax.experimental.pallas import tpu as pltpu
from jax.sharding import PartitionSpec as P

WIN = 4
HEADS = 2
MASKED = -1e30
NT = (((1,), (1,)), ((), ()))
NN = (((1,), (0,)), ((), ()))
WHOLE = pl.BlockSpec(memory_space=pltpu.VMEM)
ANY = pl.BlockSpec(memory_space=pl.ANY)
SCALARS = pl.BlockSpec(memory_space=pltpu.SMEM)
BF16, F32 = jnp.bfloat16, jnp.float32

OWN, A, B, C = range(WIN)
SLOTS = {1: ((OWN, 0), (B, 0), (A, 0), (C, 0)), 2: ((OWN, None), (B, 1), (B, 0), (A, 1), (A, 0), (C, 1), (C, 0))}


def in_vmem(*arrays):
    return [pltpu.with_memory_space_constraint(x, pltpu.VMEM) for x in arrays]


def dot(a, b, dims):
    return lax.dot_general(a, b, dims, preferred_element_type=F32)


def fold(x, op):
    return op(x.reshape(x.shape[0] // 8, 8, x.shape[1]), axis=0)


def place():
    return lax.axis_index("ctx"), lax.axis_index("head")


def distances(info):
    odd = info[0] & 1
    return {OWN: 0, A: 3 - 2 * odd, B: 2, C: 1 + 2 * odd}


def moved(info, tile, shard):
    if shard not in (A, C):
        return None
    odd = info[0] & 1
    return (tile == 1) & (odd == (1 if shard == C else 0))


def tile_of(info, tiles, index):
    return index ^ info[1] if tiles == 2 else index


def stored(info, tiles, part):
    return part ^ info[1] if tiles == 2 else part


def mask_kernel(shard, lengths, *bias_refs):
    info = place()
    tiles = len(bias_refs)
    part = shard // tiles
    back = distances(info)
    for index, bias_ref in enumerate(bias_refs):
        tile = tile_of(info, tiles, index)
        first = info[0] * shard + tile * part
        query = first + lax.broadcasted_iota(jnp.int32, (1, part), 1)
        low = jnp.zeros((1, part), jnp.int32)
        start = jnp.int32(0)
        for d in range(lengths.shape[0]):
            low = jnp.where(query >= start, start, low)
            start = start + lengths[d]
        for slot, (s, j) in enumerate(SLOTS[tiles]):
            at = (info[0] - back[s]) * shard + (tile if j is None else j) * part
            if tiles == 2 and j == 0 and moved(info, tile, s) is not None:
                at = jnp.where(moved(info, tile, s), info[0] * shard, at)
            key = at + lax.broadcasted_iota(jnp.int32, (part, part), 0)
            ok = (key >= low) & (key <= query)
            bias_ref[slot * part : (slot + 1) * part, :] = jnp.where(ok, 0.0, MASKED)


def fill(info, tiles, tile, shard_refs, slots, k_ref=None, v_ref=None):
    shard, width = shard_refs[0].shape
    part, hd = shard // tiles, width // 2

    def rows(s, j):
        return shard_refs[s][pl.ds(pl.multiple_of(stored(info, tiles, j) * part, part), part), :]

    for slot in slots:
        s, j = SLOTS[tiles][slot]
        x = rows(s, tile if j is None else j)
        if tiles == 2 and j == 0 and moved(info, tile, s) is not None:
            x = jnp.where(moved(info, tile, s), rows(OWN, 0), x)
        at = slice(slot * part, (slot + 1) * part)
        if k_ref is not None:
            k_ref[at, :] = x[:, :hd]
        if v_ref is not None:
            v_ref[at, :] = x[:, hd:]


def attend_kernel(tiles, index, *refs):
    info = place()
    last = index == tiles - 1
    sources, refs = (refs[:1], refs[1:]) if last else (refs[:2], refs[2:])
    bias_ref, *refs = refs
    shard_refs, refs = refs[:WIN], refs[WIN:]
    acc_refs = []
    if index:
        acc_refs, refs = [refs[0]], refs[2:]
    out_hbm, ds_ref, *refs = refs
    if last:
        grad_refs, refs = refs[:WIN], refs[WIN:]
        acc_refs.append(refs[0])
    else:
        acc_refs.append(refs[0])
    acc_ref, k_ref, v_ref, vt_ref, p_ref, out_ref, sem = refs

    shard, width = shard_refs[0].shape
    hd = width // 2
    keys, rows = bias_ref.shape
    columns = out_hbm.shape[1]
    pairs = columns // hd // HEADS
    part = shard // tiles
    tile = tile_of(info, tiles, index)
    n = HEADS * rows
    log2e = math.log2(math.e) / math.sqrt(hd)
    scaling = 1 / math.sqrt(hd)
    fill(info, tiles, tile, shard_refs, range(len(SLOTS[tiles])), k_ref, v_ref)
    vt_ref[...] = v_ref[...].T

    def at(p):
        return slice(p * n, (p + 1) * n)

    if last:
        q_do = [(sources[0], 0), (sources[0], columns)]
    else:
        q_do = [(source, pl.multiple_of(info[1] * columns, 128)) for source in sources]

    def rows_of(p):
        heads = range(p * HEADS, (p + 1) * HEADS)
        return [jnp.concatenate([x[:, pl.ds(start + h * hd, hd)] for h in heads], axis=0) for x, start in q_do]

    def scores(p):
        s = dot(k_ref[...], rows_of(p)[0], NT) + jnp.concatenate([bias_ref[...]] * HEADS, axis=1)
        return s, jnp.max(fold(s, jnp.max), axis=0, keepdims=True)

    def weights(p, s, top):
        e = jnp.exp2((s - top) * log2e)
        total = jnp.sum(fold(e, jnp.sum), axis=0, keepdims=True)
        p_f32 = e * (1.0 / total)
        p_ref[:, at(p)] = p_f32.astype(BF16)
        return p_f32

    def outputs(p):
        out = dot(vt_ref[...], p_ref[:, at(p)], NN).astype(BF16)
        do_t = rows_of(p)[1].T.astype(F32)
        delta = jnp.sum(do_t * out.astype(F32), axis=0, keepdims=True)
        for i in range(HEADS):
            h = p * HEADS + i
            out_ref[:, h * hd : (h + 1) * hd] = out[:, i * rows : (i + 1) * rows].T
        here = slice(p * HEADS * hd, (p + 1) * HEADS * hd)
        there = pl.ds(pl.multiple_of(tile * rows, rows), rows)
        copy = pltpu.make_async_copy(out_ref.at[:, here], out_hbm.at[there, here], sem.at[p])
        copy.start()
        stores.append(copy)
        return delta

    def dprobs(p):
        return dot(v_ref[...], rows_of(p)[1], NT)

    def dscores(p, w, dp, delta):
        ds_ref[:, at(p)] = (w * (dp - delta)).astype(BF16)

    def sums(p):
        q, do = rows_of(p)
        dk, dv = dot(ds_ref[:, at(p)], q, NN), dot(p_ref[:, at(p)], do, NN)
        if p:
            acc_ref[:, :hd] += dk
            acc_ref[:, hd:] += dv
        else:
            acc_ref[:, :hd], acc_ref[:, hd:] = dk, dv

    stores = []
    w = weights(0, *scores(0))
    for p in range(pairs):
        following = scores(p + 1) if p + 1 < pairs else None
        dp = dprobs(p)
        delta = outputs(p)
        if p:
            sums(p - 1)
        nw = weights(p + 1, *following) if p + 1 < pairs else None
        dscores(p, w, dp, delta)
        w = nw
    sums(pairs - 1)
    if last:

        def give(ref, row, x):
            where = pl.ds(pl.multiple_of(row * part, part), part)
            ref[where, :hd] = (x[:, :hd] * scaling).astype(ref.dtype)
            ref[where, hd:] = x[:, hd:].astype(ref.dtype)

        parts = [[acc[slot * part : (slot + 1) * part, :] for acc in acc_refs] for slot in range(len(SLOTS[tiles]))]
        own = list(parts[0])
        for (s, j), xs in list(zip(SLOTS[tiles], parts))[1:]:
            if tiles == 2 and j == 0 and s in (A, C):
                for i, x in enumerate(xs):
                    keep = jnp.where(moved(info, tile_of(info, tiles, i), s), 0.0, 1.0)
                    own[1 - i] = own[1 - i] + x * (1.0 - keep)
                    xs[i] = x * keep
            give(grad_refs[s], stored(info, tiles, j), sum(xs[1:], xs[0]))
        for i, x in enumerate(own):
            give(grad_refs[OWN], i, x)
    for copy in stores:
        copy.wait()


def queries_kernel(tiles, *refs):
    info = place()
    shard_refs, refs = refs[:WIN], refs[WIN:]
    ds_refs, (dq_hbm, k_ref, kt_ref, dq_ref, sem) = refs[:tiles], refs[tiles:]
    hd, keys = kt_ref.shape
    rows = dq_hbm.shape[0] // tiles
    n = HEADS * rows
    width = HEADS * hd
    stores = []
    for index, ds_ref in enumerate(ds_refs):
        tile = tile_of(info, tiles, index)
        fill(info, tiles, tile, shard_refs, range(len(SLOTS[tiles])), k_ref)
        kt_ref[...] = k_ref[...].T
        for p in range(ds_ref.shape[1] // n):
            dq = (dot(kt_ref[...], ds_ref[:, p * n : (p + 1) * n], NN) * (1 / math.sqrt(hd))).astype(BF16)
            for i in range(HEADS):
                here = slice(p * width + i * hd, p * width + (i + 1) * hd)
                dq_ref[index * rows : (index + 1) * rows, here] = dq[:, i * rows : (i + 1) * rows].T
            here = slice(p * width, (p + 1) * width)
            there = pl.ds(pl.multiple_of(tile * rows, rows), rows)
            source = dq_ref.at[index * rows : (index + 1) * rows, here]
            copy = pltpu.make_async_copy(source, dq_hbm.at[there, here], sem.at[len(stores)])
            copy.start()
            stores.append(copy)
    for copy in stores:
        copy.wait()


def params(mib):
    return pltpu.CompilerParams(vmem_limit_bytes=mib << 20)


def masks(doc_lengths, shard, tiles):
    part = shard // tiles
    return pl.pallas_call(
        functools.partial(mask_kernel, shard),
        out_shape=[pltpu.VMEM((len(SLOTS[tiles]) * part, part), F32)] * tiles,
        in_specs=[SCALARS],
        out_specs=[WHOLE] * tiles,
        compiler_params=params(4),
        name="masks",
    )(doc_lengths)


def attend(q_do, bias, shards, before, tiles, columns):
    shard, width = shards[0].shape
    hd = width // 2
    index = 0 if before is None else 1
    last = index == tiles - 1
    keys, rows = bias.shape
    all_rows = columns // hd * rows
    acc = pltpu.VMEM((keys, width), F32)
    args = in_vmem(*q_do, bias, *shards)
    in_specs = [WHOLE] * len(args)
    aliases = {}
    if before is not None:
        aliases = {len(args) + 1: 0}
        args += [*in_vmem(before[0]), before[1]]
        in_specs += [WHOLE, ANY]
    out_shape = [jax.ShapeDtypeStruct((shard, columns), BF16), pltpu.VMEM((keys, all_rows), BF16)]
    if last:
        out_shape += [pltpu.VMEM((shard, width), d) for d in (F32, BF16, F32, BF16)]
    else:
        out_shape += [acc]
    return pl.pallas_call(
        functools.partial(attend_kernel, tiles, index),
        out_shape=out_shape,
        in_specs=in_specs,
        out_specs=[ANY] + [WHOLE] * (len(out_shape) - 1),
        scratch_shapes=[
            *([acc] if last else []),
            pltpu.VMEM((keys, hd), BF16),
            pltpu.VMEM((keys, hd), BF16),
            pltpu.VMEM((hd, keys), BF16),
            pltpu.VMEM((keys, all_rows), BF16),
            pltpu.VMEM((rows, columns), BF16),
            pltpu.SemaphoreType.DMA((columns // hd // HEADS,)),
        ],
        input_output_aliases=aliases,
        compiler_params=params(24),
        cost_estimate=pl.CostEstimate(
            flops=10 * keys * rows * columns, transcendentals=keys * all_rows, bytes_accessed=1 << 21
        ),
        name="attend_last" if last else "attend_first",
    )(*args)


def query_gradients(shards, dscores, columns):
    shard, width = shards[0].shape
    tiles = len(dscores)
    hd, keys = width // 2, dscores[0].shape[0]
    return pl.pallas_call(
        functools.partial(queries_kernel, tiles),
        out_shape=jax.ShapeDtypeStruct((shard, columns), BF16),
        in_specs=[WHOLE] * (WIN + tiles),
        out_specs=ANY,
        scratch_shapes=[
            pltpu.VMEM((keys, hd), BF16),
            pltpu.VMEM((hd, keys), BF16),
            pltpu.VMEM((shard, columns), BF16),
            pltpu.SemaphoreType.DMA((tiles * (columns // hd // HEADS),)),
        ],
        compiler_params=params(12),
        cost_estimate=pl.CostEstimate(flops=2 * keys * shard * columns, transcendentals=0, bytes_accessed=1 << 21),
        name="query_gradients",
    )(*in_vmem(*shards, *dscores))


def gather_kernel(own_ref, *refs):
    total = own_ref[...]
    for r in refs[:-2]:
        total = total + r[...].astype(F32)
    hd = refs[-1].shape[1]
    refs[-2][...] = total[:, :hd].astype(BF16)
    refs[-1][...] = total[:, hd:].astype(BF16)


def in_order_kernel(own_ref, *refs):
    info = place()
    near, (k_ref, v_ref) = refs[:-2], refs[-2:]
    shard, hd = k_ref.shape
    part = shard // 2
    total = own_ref[...]
    for r in near:
        total = total + r[...].astype(F32)
    for j in range(2):
        to = pl.ds(pl.multiple_of((j ^ info[1]) * part, part), part)
        k_ref[to, :] = total[j * part : (j + 1) * part, :hd].astype(BF16)
        v_ref[to, :] = total[j * part : (j + 1) * part, hd:].astype(BF16)


def move(value, kind, back=False):
    count = lax.axis_size("ctx")
    steps = {A: lambda i: 3 if i % 2 else 1, B: lambda i: 2, C: lambda i: -1 if i % 2 else 1}[kind]
    pairs = [(i, (i + steps(i)) % count) for i in range(count)]
    return lax.ppermute(value, "ctx", [p[::-1] for p in pairs] if back else pairs)


def window(own, bias):
    b = move(own, B)
    a = move(own, A)
    b, *bias = lax.optimization_barrier((b, *bias))
    return [own, a, b, move(b, C)], bias


def body(queries, keys, values, d_out, doc_lengths):
    count = lax.axis_size("head")
    head = lax.axis_index("head")
    shard = count * queries.shape[0]
    hd = keys.shape[1] // count
    columns = queries.shape[1] // count
    tiles = 2 if count == 2 else 1
    bias = masks(doc_lengths, shard, tiles)
    if tiles == 2:
        other = 1 - head

        def half(x, index):
            width = x.shape[1] // 2
            return lax.dynamic_slice_in_dim(x, index * width, width, 1)

        def key_value(index):
            return jnp.concatenate([half(keys, index), half(values, index)], axis=1)

        def swap(x):
            return lax.ppermute(x, "head", [(0, 1), (1, 0)])

        own = jnp.concatenate([key_value(head), swap(key_value(other))], axis=0)
        both = swap(jnp.concatenate([half(queries, other), half(d_out, other)], axis=1))
        shards, bias = window(own, bias)
        out, ds_first, acc = attend((queries, d_out), bias[0], shards, None, 2, columns)
        out, ds_last, *grads = attend((both,), bias[1], shards, (acc, out), 2, columns)
        dscores = (ds_first, ds_last)
    else:
        swap = lambda x: lax.all_to_all(x, "head", split_axis=1, concat_axis=0, tiled=True)
        own = jnp.concatenate([swap(keys), swap(values)], axis=1)
        both = jnp.concatenate([swap(queries), swap(d_out)], axis=1)
        shards, bias = window(own, bias)
        out, ds_last, *grads = attend((both,), bias[0], shards, None, 1, columns)
        dscores = (ds_last,)
    from_c = move(grads[C], C, True)
    near_a = move(grads[A], A, True)
    near_b = move((grads[B] + from_c.astype(F32)).astype(BF16), B, True)
    dq = query_gradients(shards, dscores, columns)
    grad_keys, grad_values = pl.pallas_call(
        in_order_kernel if tiles == 2 else gather_kernel,
        out_shape=[jax.ShapeDtypeStruct((shard, hd), BF16)] * 2,
        in_specs=[WHOLE] * 3,
        out_specs=[WHOLE] * 2,
        compiler_params=params(4),
        name="gather",
    )(*in_vmem(grads[OWN], near_a, near_b))
    return out, dq, grad_keys, grad_values


def solution(mesh):
    rows = P(("ctx", "head"), None)
    return jax.shard_map(
        body,
        mesh=mesh,
        in_specs=(rows, rows, rows, rows, P()),
        out_specs=(P("ctx", "head"),) * 4,
        check_vma=False,
    )
```

```python
import functools
import math

import jax
import jax.numpy as jnp
from jax import lax
from jax.experimental import pallas as pl
from jax.experimental.pallas import tpu as pltpu
from jax.sharding import PartitionSpec as P

WIN = 4
HEADS = 2
MASKED = -1e30
NT = (((1,), (1,)), ((), ()))
NN = (((1,), (0,)), ((), ()))
WHOLE = pl.BlockSpec(memory_space=pltpu.VMEM)
ANY = pl.BlockSpec(memory_space=pl.ANY)
SCALARS = pl.BlockSpec(memory_space=pltpu.SMEM)
BF16, F32 = jnp.bfloat16, jnp.float32

OWN, A, B, C = range(WIN)
SLOTS = {1: ((OWN, 0), (B, 0), (A, 0), (C, 0)), 2: ((OWN, None), (B, 1), (B, 0), (A, 1), (A, 0), (C, 1), (C, 0))}


def in_vmem(*arrays):
    return [pltpu.with_memory_space_constraint(x, pltpu.VMEM) for x in arrays]


def dot(a, b, dims):
    return lax.dot_general(a, b, dims, preferred_element_type=F32)


def fold(x, op):
    return op(x.reshape(x.shape[0] // 8, 8, x.shape[1]), axis=0)


def place():
    return lax.axis_index("ctx"), lax.axis_index("head")


def distances(info):
    odd = info[0] & 1
    return {OWN: 0, A: 3 - 2 * odd, B: 2, C: 1 + 2 * odd}


def moved(info, tile, shard):
    if shard not in (A, C):
        return None
    odd = info[0] & 1
    return (tile == 1) & (odd == (1 if shard == C else 0))


def tile_of(info, tiles, index):
    return index ^ info[1] if tiles == 2 else index


def stored(info, tiles, part):
    return part ^ info[1] if tiles == 2 else part


def mask_kernel(shard, lengths, *bias_refs):
    info = place()
    tiles = len(bias_refs)
    part = shard // tiles
    back = distances(info)
    for index, bias_ref in enumerate(bias_refs):
        tile = tile_of(info, tiles, index)
        first = info[0] * shard + tile * part
        query = first + lax.broadcasted_iota(jnp.int32, (1, part), 1)
        low = jnp.zeros((1, part), jnp.int32)
        start = jnp.int32(0)
        for d in range(lengths.shape[0]):
            low = jnp.where(query >= start, start, low)
            start = start + lengths[d]
        for slot, (s, j) in enumerate(SLOTS[tiles]):
            at = (info[0] - back[s]) * shard + (tile if j is None else j) * part
            if tiles == 2 and j == 0 and moved(info, tile, s) is not None:
                at = jnp.where(moved(info, tile, s), info[0] * shard, at)
            key = at + lax.broadcasted_iota(jnp.int32, (part, part), 0)
            ok = (key >= low) & (key <= query)
            bias_ref[slot * part : (slot + 1) * part, :] = jnp.where(ok, 0.0, MASKED)


def fill(info, tiles, tile, shard_refs, slots, k_ref=None, v_ref=None):
    shard, width = shard_refs[0].shape
    part, hd = shard // tiles, width // 2

    def rows(s, j):
        return shard_refs[s][pl.ds(pl.multiple_of(stored(info, tiles, j) * part, part), part), :]

    for slot in slots:
        s, j = SLOTS[tiles][slot]
        x = rows(s, tile if j is None else j)
        if tiles == 2 and j == 0 and moved(info, tile, s) is not None:
            x = jnp.where(moved(info, tile, s), rows(OWN, 0), x)
        at = slice(slot * part, (slot + 1) * part)
        if k_ref is not None:
            k_ref[at, :] = x[:, :hd]
        if v_ref is not None:
            v_ref[at, :] = x[:, hd:]


def attend_kernel(tiles, index, *refs):
    info = place()
    last = index == tiles - 1
    sources, refs = (refs[:1], refs[1:]) if last else (refs[:2], refs[2:])
    bias_ref, *refs = refs
    shard_refs, refs = refs[:WIN], refs[WIN:]
    acc_refs = []
    if index:
        acc_refs, refs = [refs[0]], refs[2:]
    out_hbm, ds_ref, *refs = refs
    if last:
        grad_refs, refs = refs[:WIN], refs[WIN:]
        acc_refs.append(refs[0])
    else:
        acc_refs.append(refs[0])
    acc_ref, k_ref, v_ref, vt_ref, p_ref, out_ref, sem = refs

    shard, width = shard_refs[0].shape
    hd = width // 2
    keys, rows = bias_ref.shape
    columns = out_hbm.shape[1]
    pairs = columns // hd // HEADS
    part = shard // tiles
    tile = tile_of(info, tiles, index)
    n = HEADS * rows
    log2e = math.log2(math.e) / math.sqrt(hd)
    scaling = 1 / math.sqrt(hd)
    fill(info, tiles, tile, shard_refs, range(len(SLOTS[tiles])), k_ref, v_ref)
    vt_ref[...] = v_ref[...].T

    def at(p):
        return slice(p * n, (p + 1) * n)

    if last:
        q_do = [(sources[0], 0), (sources[0], columns)]
    else:
        q_do = [(source, pl.multiple_of(info[1] * columns, 128)) for source in sources]

    @functools.cache
    def rows_of(p):
        heads = range(p * HEADS, (p + 1) * HEADS)
        return [jnp.concatenate([x[:, pl.ds(start + h * hd, hd)] for h in heads], axis=0) for x, start in q_do]

    def scores(p):
        s = dot(k_ref[...], rows_of(p)[0], NT) + jnp.concatenate([bias_ref[...]] * HEADS, axis=1)
        return s, jnp.max(fold(s, jnp.max), axis=0, keepdims=True)

    def weights(p, s, top):
        e = jnp.exp2((s - top) * log2e)
        total = jnp.sum(fold(e, jnp.sum), axis=0, keepdims=True)
        p_f32 = e * (1.0 / total)
        p_ref[:, at(p)] = p_f32.astype(BF16)
        return p_f32

    def outputs(p):
        out = dot(vt_ref[...], p_ref[:, at(p)], NN).astype(BF16)
        do_t = rows_of(p)[1].T.astype(F32)
        delta = jnp.sum(do_t * out.astype(F32), axis=0, keepdims=True)
        for i in range(HEADS):
            h = p * HEADS + i
            out_ref[:, h * hd : (h + 1) * hd] = out[:, i * rows : (i + 1) * rows].T
        here = slice(p * HEADS * hd, (p + 1) * HEADS * hd)
        there = pl.ds(pl.multiple_of(tile * rows, rows), rows)
        copy = pltpu.make_async_copy(out_ref.at[:, here], out_hbm.at[there, here], sem.at[p])
        copy.start()
        stores.append(copy)
        return delta

    def dprobs(p):
        return dot(v_ref[...], rows_of(p)[1], NT)

    def dscores(p, w, dp, delta):
        ds_ref[:, at(p)] = (w * (dp - delta)).astype(BF16)

    def sums(p):
        q, do = rows_of(p)
        dk, dv = dot(ds_ref[:, at(p)], q, NN), dot(p_ref[:, at(p)], do, NN)
        if p:
            acc_ref[:, :hd] += dk
            acc_ref[:, hd:] += dv
        else:
            acc_ref[:, :hd], acc_ref[:, hd:] = dk, dv

    stores = []
    w = weights(0, *scores(0))
    for p in range(pairs):
        following = scores(p + 1) if p + 1 < pairs else None
        dp = dprobs(p)
        delta = outputs(p)
        if p:
            sums(p - 1)
        nw = weights(p + 1, *following) if p + 1 < pairs else None
        dscores(p, w, dp, delta)
        w = nw
    sums(pairs - 1)
    if last:

        def give(ref, row, x):
            where = pl.ds(pl.multiple_of(row * part, part), part)
            ref[where, :hd] = (x[:, :hd] * scaling).astype(ref.dtype)
            ref[where, hd:] = x[:, hd:].astype(ref.dtype)

        parts = [[acc[slot * part : (slot + 1) * part, :] for acc in acc_refs] for slot in range(len(SLOTS[tiles]))]
        own = list(parts[0])
        for (s, j), xs in list(zip(SLOTS[tiles], parts))[1:]:
            if tiles == 2 and j == 0 and s in (A, C):
                for i, x in enumerate(xs):
                    keep = jnp.where(moved(info, tile_of(info, tiles, i), s), 0.0, 1.0)
                    own[1 - i] = own[1 - i] + x * (1.0 - keep)
                    xs[i] = x * keep
            give(grad_refs[s], stored(info, tiles, j), sum(xs[1:], xs[0]))
        for i, x in enumerate(own):
            give(grad_refs[OWN], i, x)
    for copy in stores:
        copy.wait()


def queries_kernel(tiles, *refs):
    info = place()
    shard_refs, refs = refs[:WIN], refs[WIN:]
    ds_refs, (dq_hbm, k_ref, kt_ref, dq_ref, sem) = refs[:tiles], refs[tiles:]
    hd, keys = kt_ref.shape
    rows = dq_hbm.shape[0] // tiles
    n = HEADS * rows
    width = HEADS * hd
    stores = []
    for index, ds_ref in enumerate(ds_refs):
        tile = tile_of(info, tiles, index)
        fill(info, tiles, tile, shard_refs, range(len(SLOTS[tiles])), k_ref)
        kt_ref[...] = k_ref[...].T
        for p in range(ds_ref.shape[1] // n):
            dq = (dot(kt_ref[...], ds_ref[:, p * n : (p + 1) * n], NN) * (1 / math.sqrt(hd))).astype(BF16)
            for i in range(HEADS):
                here = slice(p * width + i * hd, p * width + (i + 1) * hd)
                dq_ref[index * rows : (index + 1) * rows, here] = dq[:, i * rows : (i + 1) * rows].T
            here = slice(p * width, (p + 1) * width)
            there = pl.ds(pl.multiple_of(tile * rows, rows), rows)
            source = dq_ref.at[index * rows : (index + 1) * rows, here]
            copy = pltpu.make_async_copy(source, dq_hbm.at[there, here], sem.at[len(stores)])
            copy.start()
            stores.append(copy)
    for copy in stores:
        copy.wait()


def params(mib):
    return pltpu.CompilerParams(vmem_limit_bytes=mib << 20)


def masks(doc_lengths, shard, tiles):
    part = shard // tiles
    return pl.pallas_call(
        functools.partial(mask_kernel, shard),
        out_shape=[pltpu.VMEM((len(SLOTS[tiles]) * part, part), F32)] * tiles,
        in_specs=[SCALARS],
        out_specs=[WHOLE] * tiles,
        compiler_params=params(4),
        name="masks",
    )(doc_lengths)


def attend(q_do, bias, shards, before, tiles, columns):
    shard, width = shards[0].shape
    hd = width // 2
    index = 0 if before is None else 1
    last = index == tiles - 1
    keys, rows = bias.shape
    all_rows = columns // hd * rows
    acc = pltpu.VMEM((keys, width), F32)
    args = in_vmem(*q_do, bias, *shards)
    in_specs = [WHOLE] * len(args)
    aliases = {}
    if before is not None:
        aliases = {len(args) + 1: 0}
        args += [*in_vmem(before[0]), before[1]]
        in_specs += [WHOLE, ANY]
    out_shape = [jax.ShapeDtypeStruct((shard, columns), BF16), pltpu.VMEM((keys, all_rows), BF16)]
    if last:
        out_shape += [pltpu.VMEM((shard, width), d) for d in (F32, BF16, F32, BF16)]
    else:
        out_shape += [acc]
    return pl.pallas_call(
        functools.partial(attend_kernel, tiles, index),
        out_shape=out_shape,
        in_specs=in_specs,
        out_specs=[ANY] + [WHOLE] * (len(out_shape) - 1),
        scratch_shapes=[
            *([acc] if last else []),
            pltpu.VMEM((keys, hd), BF16),
            pltpu.VMEM((keys, hd), BF16),
            pltpu.VMEM((hd, keys), BF16),
            pltpu.VMEM((keys, all_rows), BF16),
            pltpu.VMEM((rows, columns), BF16),
            pltpu.SemaphoreType.DMA((columns // hd // HEADS,)),
        ],
        input_output_aliases=aliases,
        compiler_params=params(24),
        cost_estimate=pl.CostEstimate(
            flops=10 * keys * rows * columns, transcendentals=keys * all_rows, bytes_accessed=1 << 21
        ),
        name="attend_last" if last else "attend_first",
    )(*args)


def query_gradients(shards, dscores, columns):
    shard, width = shards[0].shape
    tiles = len(dscores)
    hd, keys = width // 2, dscores[0].shape[0]
    return pl.pallas_call(
        functools.partial(queries_kernel, tiles),
        out_shape=jax.ShapeDtypeStruct((shard, columns), BF16),
        in_specs=[WHOLE] * (WIN + tiles),
        out_specs=ANY,
        scratch_shapes=[
            pltpu.VMEM((keys, hd), BF16),
            pltpu.VMEM((hd, keys), BF16),
            pltpu.VMEM((shard, columns), BF16),
            pltpu.SemaphoreType.DMA((tiles * (columns // hd // HEADS),)),
        ],
        compiler_params=params(12),
        cost_estimate=pl.CostEstimate(flops=2 * keys * shard * columns, transcendentals=0, bytes_accessed=1 << 21),
        name="query_gradients",
    )(*in_vmem(*shards, *dscores))


def gather_kernel(own_ref, *refs):
    total = own_ref[...]
    for r in refs[:-2]:
        total = total + r[...].astype(F32)
    hd = refs[-1].shape[1]
    refs[-2][...] = total[:, :hd].astype(BF16)
    refs[-1][...] = total[:, hd:].astype(BF16)


def in_order_kernel(own_ref, *refs):
    info = place()
    near, (k_ref, v_ref) = refs[:-2], refs[-2:]
    shard, hd = k_ref.shape
    part = shard // 2
    total = own_ref[...]
    for r in near:
        total = total + r[...].astype(F32)
    for j in range(2):
        to = pl.ds(pl.multiple_of((j ^ info[1]) * part, part), part)
        k_ref[to, :] = total[j * part : (j + 1) * part, :hd].astype(BF16)
        v_ref[to, :] = total[j * part : (j + 1) * part, hd:].astype(BF16)


def move(value, kind, back=False):
    count = lax.axis_size("ctx")
    steps = {A: lambda i: 3 if i % 2 else 1, B: lambda i: 2, C: lambda i: -1 if i % 2 else 1}[kind]
    pairs = [(i, (i + steps(i)) % count) for i in range(count)]
    return lax.ppermute(value, "ctx", [p[::-1] for p in pairs] if back else pairs)


def window(own, bias):
    a = move(own, A)
    b = move(own, B)
    a, b = lax.optimization_barrier((a, b))
    b, *bias = lax.optimization_barrier((b, *bias))
    return [own, a, b, move(b, C)], bias


def body(queries, keys, values, d_out, doc_lengths):
    count = lax.axis_size("head")
    head = lax.axis_index("head")
    shard = count * queries.shape[0]
    hd = keys.shape[1] // count
    columns = queries.shape[1] // count
    tiles = 2 if count == 2 else 1
    bias = masks(doc_lengths, shard, tiles)
    if tiles == 2:
        other = 1 - head

        def half(x, index):
            width = x.shape[1] // 2
            return lax.dynamic_slice_in_dim(x, index * width, width, 1)

        def key_value(index):
            return jnp.concatenate([half(keys, index), half(values, index)], axis=1)

        def swap(x):
            return lax.ppermute(x, "head", [(0, 1), (1, 0)])

        own = jnp.concatenate([key_value(head), swap(key_value(other))], axis=0)
        both = swap(jnp.concatenate([half(queries, other), half(d_out, other)], axis=1))
        shards, bias = window(own, bias)
        out, ds_first, acc = attend((queries, d_out), bias[0], shards, None, 2, columns)
        out, ds_last, *grads = attend((both,), bias[1], shards, (acc, out), 2, columns)
        dscores = (ds_first, ds_last)
    else:
        swap = lambda x: lax.all_to_all(x, "head", split_axis=1, concat_axis=0, tiled=True)
        own = jnp.concatenate([swap(keys), swap(values)], axis=1)
        both = jnp.concatenate([swap(queries), swap(d_out)], axis=1)
        shards, bias = window(own, bias)
        out, ds_last, *grads = attend((both,), bias[0], shards, None, 1, columns)
        dscores = (ds_last,)
    from_c = move(grads[C], C, True)
    near_a = move(grads[A], A, True)
    near_b = move((grads[B] + from_c.astype(F32)).astype(BF16), B, True)
    dq = query_gradients(shards, dscores, columns)
    grad_keys, grad_values = pl.pallas_call(
        in_order_kernel if tiles == 2 else gather_kernel,
        out_shape=[jax.ShapeDtypeStruct((shard, hd), BF16)] * 2,
        in_specs=[WHOLE] * 3,
        out_specs=[WHOLE] * 2,
        compiler_params=params(4),
        name="gather",
    )(*in_vmem(grads[OWN], near_a, near_b))
    return out, dq, grad_keys, grad_values


def solution(mesh):
    rows = P(("ctx", "head"), None)
    return jax.shard_map(
        body,
        mesh=mesh,
        in_specs=(rows, rows, rows, rows, P()),
        out_specs=(P("ctx", "head"),) * 4,
        check_vma=False,
    )
```

```python
import functools
import math

import jax
import jax.numpy as jnp
from jax import lax
from jax.experimental import pallas as pl
from jax.experimental.pallas import tpu as pltpu
from jax.sharding import PartitionSpec as P

WIN = 4
HEADS = 2
MASKED = -1e30
NT = (((1,), (1,)), ((), ()))
NN = (((1,), (0,)), ((), ()))
WHOLE = pl.BlockSpec(memory_space=pltpu.VMEM)
ANY = pl.BlockSpec(memory_space=pl.ANY)
SCALARS = pl.BlockSpec(memory_space=pltpu.SMEM)
BF16, F32 = jnp.bfloat16, jnp.float32

OWN, A, B, C = range(WIN)
SLOTS = {1: ((OWN, 0), (B, 0), (A, 0), (C, 0)), 2: ((OWN, None), (B, 1), (B, 0), (A, 1), (A, 0), (C, 1), (C, 0))}


def in_vmem(*arrays):
    return [pltpu.with_memory_space_constraint(x, pltpu.VMEM) for x in arrays]


def dot(a, b, dims):
    return lax.dot_general(a, b, dims, preferred_element_type=F32)


def fold(x, op):
    return op(x.reshape(x.shape[0] // 8, 8, x.shape[1]), axis=0)


def place():
    return lax.axis_index("ctx"), lax.axis_index("head")


def distances(info):
    odd = info[0] & 1
    return {OWN: 0, A: 3 - 2 * odd, B: 2, C: 1 + 2 * odd}


def moved(info, tile, shard):
    if shard not in (A, C):
        return None
    odd = info[0] & 1
    return (tile == 1) & (odd == (1 if shard == C else 0))


def tile_of(info, tiles, index):
    return index ^ info[1] if tiles == 2 else index


def stored(info, tiles, part):
    return part ^ info[1] if tiles == 2 else part


def mask_kernel(shard, lengths, *bias_refs):
    info = place()
    tiles = len(bias_refs)
    part = shard // tiles
    back = distances(info)
    for index, bias_ref in enumerate(bias_refs):
        tile = tile_of(info, tiles, index)
        first = info[0] * shard + tile * part
        query = first + lax.broadcasted_iota(jnp.int32, (1, part), 1)
        low = jnp.zeros((1, part), jnp.int32)
        start = jnp.int32(0)
        for d in range(lengths.shape[0]):
            low = jnp.where(query >= start, start, low)
            start = start + lengths[d]
        for slot, (s, j) in enumerate(SLOTS[tiles]):
            at = (info[0] - back[s]) * shard + (tile if j is None else j) * part
            if tiles == 2 and j == 0 and moved(info, tile, s) is not None:
                at = jnp.where(moved(info, tile, s), info[0] * shard, at)
            key = at + lax.broadcasted_iota(jnp.int32, (part, part), 0)
            ok = (key >= low) & (key <= query)
            bias_ref[slot * part : (slot + 1) * part, :] = jnp.where(ok, 0.0, MASKED)


def fill(info, tiles, tile, shard_refs, slots, k_ref=None, v_ref=None):
    shard, width = shard_refs[0].shape
    part, hd = shard // tiles, width // 2

    def rows(s, j):
        return shard_refs[s][pl.ds(pl.multiple_of(stored(info, tiles, j) * part, part), part), :]

    for slot in slots:
        s, j = SLOTS[tiles][slot]
        x = rows(s, tile if j is None else j)
        if tiles == 2 and j == 0 and moved(info, tile, s) is not None:
            x = jnp.where(moved(info, tile, s), rows(OWN, 0), x)
        at = slice(slot * part, (slot + 1) * part)
        if k_ref is not None:
            k_ref[at, :] = x[:, :hd]
        if v_ref is not None:
            v_ref[at, :] = x[:, hd:]


def attend_kernel(tiles, index, *refs):
    info = place()
    last = index == tiles - 1
    sources, refs = (refs[:1], refs[1:]) if last else (refs[:2], refs[2:])
    bias_ref, *refs = refs
    shard_refs, refs = refs[:WIN], refs[WIN:]
    acc_refs = []
    if index:
        acc_refs, refs = [refs[0]], refs[2:]
    out_hbm, ds_ref, *refs = refs
    if last:
        grad_refs, refs = refs[:WIN], refs[WIN:]
        acc_refs.append(refs[0])
    else:
        acc_refs.append(refs[0])
    acc_ref, k_ref, v_ref, vt_ref, p_ref, out_ref, sem = refs

    shard, width = shard_refs[0].shape
    hd = width // 2
    keys, rows = bias_ref.shape
    columns = out_hbm.shape[1]
    pairs = columns // hd // HEADS
    part = shard // tiles
    tile = tile_of(info, tiles, index)
    n = HEADS * rows
    log2e = math.log2(math.e) / math.sqrt(hd)
    scaling = 1 / math.sqrt(hd)
    fill(info, tiles, tile, shard_refs, range(len(SLOTS[tiles])), k_ref, v_ref)
    vt_ref[...] = v_ref[...].T

    def at(p):
        return slice(p * n, (p + 1) * n)

    if last:
        q_do = [(sources[0], 0), (sources[0], columns)]
    else:
        q_do = [(source, pl.multiple_of(info[1] * columns, 128)) for source in sources]

    @functools.cache
    def rows_of(p):
        heads = range(p * HEADS, (p + 1) * HEADS)
        return [jnp.concatenate([x[:, pl.ds(start + h * hd, hd)] for h in heads], axis=0) for x, start in q_do]

    def scores(p):
        s = dot(k_ref[...], rows_of(p)[0], NT) + jnp.concatenate([bias_ref[...]] * HEADS, axis=1)
        return s, jnp.max(fold(s, jnp.max), axis=0, keepdims=True)

    def weights(p, s, top):
        e = jnp.exp2((s - top) * log2e)
        total = jnp.sum(fold(e, jnp.sum), axis=0, keepdims=True)
        p_f32 = e * (1.0 / total)
        p_ref[:, at(p)] = p_f32.astype(BF16)
        return p_f32

    def outputs(p):
        out = dot(vt_ref[...], p_ref[:, at(p)], NN).astype(BF16)
        do_t = rows_of(p)[1].T.astype(F32)
        delta = jnp.sum(do_t * out.astype(F32), axis=0, keepdims=True)
        for i in range(HEADS):
            h = p * HEADS + i
            out_ref[:, h * hd : (h + 1) * hd] = out[:, i * rows : (i + 1) * rows].T
        here = slice(p * HEADS * hd, (p + 1) * HEADS * hd)
        there = pl.ds(pl.multiple_of(tile * rows, rows), rows)
        copy = pltpu.make_async_copy(out_ref.at[:, here], out_hbm.at[there, here], sem.at[p])
        copy.start()
        stores.append(copy)
        return delta

    def dprobs(p):
        return dot(v_ref[...], rows_of(p)[1], NT)

    def dscores(p, w, dp, delta):
        ds_ref[:, at(p)] = (w * (dp - delta)).astype(BF16)

    def sums(p):
        q, do = rows_of(p)
        dk, dv = dot(ds_ref[:, at(p)], q, NN), dot(p_ref[:, at(p)], do, NN)
        if p:
            acc_ref[:, :hd] += dk
            acc_ref[:, hd:] += dv
        else:
            acc_ref[:, :hd], acc_ref[:, hd:] = dk, dv

    stores = []
    w = weights(0, *scores(0))
    for p in range(pairs):
        following = scores(p + 1) if p + 1 < pairs else None
        dp = dprobs(p)
        delta = outputs(p)
        if p:
            sums(p - 1)
        nw = weights(p + 1, *following) if p + 1 < pairs else None
        dscores(p, w, dp, delta)
        w = nw
    sums(pairs - 1)
    if last:

        def give(ref, row, x):
            where = pl.ds(pl.multiple_of(row * part, part), part)
            ref[where, :hd] = (x[:, :hd] * scaling).astype(ref.dtype)
            ref[where, hd:] = x[:, hd:].astype(ref.dtype)

        parts = [[acc[slot * part : (slot + 1) * part, :] for acc in acc_refs] for slot in range(len(SLOTS[tiles]))]
        own = list(parts[0])
        for (s, j), xs in list(zip(SLOTS[tiles], parts))[1:]:
            if tiles == 2 and j == 0 and s in (A, C):
                for i, x in enumerate(xs):
                    keep = jnp.where(moved(info, tile_of(info, tiles, i), s), 0.0, 1.0)
                    own[1 - i] = own[1 - i] + x * (1.0 - keep)
                    xs[i] = x * keep
            give(grad_refs[s], stored(info, tiles, j), sum(xs[1:], xs[0]))
        for i, x in enumerate(own):
            give(grad_refs[OWN], i, x)
    for copy in stores:
        copy.wait()


def queries_kernel(tiles, *refs):
    info = place()
    shard_refs, refs = refs[:WIN], refs[WIN:]
    ds_refs, (dq_hbm, k_ref, kt_ref, dq_ref, sem) = refs[:tiles], refs[tiles:]
    hd, keys = kt_ref.shape
    rows = dq_hbm.shape[0] // tiles
    n = HEADS * rows
    width = HEADS * hd
    stores = []
    for index, ds_ref in enumerate(ds_refs):
        tile = tile_of(info, tiles, index)
        fill(info, tiles, tile, shard_refs, range(len(SLOTS[tiles])), k_ref)
        kt_ref[...] = k_ref[...].T
        for p in range(ds_ref.shape[1] // n):
            dq = (dot(kt_ref[...], ds_ref[:, p * n : (p + 1) * n], NN) * (1 / math.sqrt(hd))).astype(BF16)
            for i in range(HEADS):
                here = slice(p * width + i * hd, p * width + (i + 1) * hd)
                dq_ref[index * rows : (index + 1) * rows, here] = dq[:, i * rows : (i + 1) * rows].T
            here = slice(p * width, (p + 1) * width)
            there = pl.ds(pl.multiple_of(tile * rows, rows), rows)
            source = dq_ref.at[index * rows : (index + 1) * rows, here]
            copy = pltpu.make_async_copy(source, dq_hbm.at[there, here], sem.at[len(stores)])
            copy.start()
            stores.append(copy)
    for copy in stores:
        copy.wait()


def params(mib):
    return pltpu.CompilerParams(vmem_limit_bytes=mib << 20)


def masks(doc_lengths, shard, tiles):
    part = shard // tiles
    return pl.pallas_call(
        functools.partial(mask_kernel, shard),
        out_shape=[pltpu.VMEM((len(SLOTS[tiles]) * part, part), F32)] * tiles,
        in_specs=[SCALARS],
        out_specs=[WHOLE] * tiles,
        compiler_params=params(4),
        name="masks",
    )(doc_lengths)


def attend(q_do, bias, shards, before, tiles, columns):
    shard, width = shards[0].shape
    hd = width // 2
    index = 0 if before is None else 1
    last = index == tiles - 1
    keys, rows = bias.shape
    all_rows = columns // hd * rows
    acc = pltpu.VMEM((keys, width), F32)
    args = in_vmem(*q_do, bias, *shards)
    in_specs = [WHOLE] * len(args)
    aliases = {}
    if before is not None:
        aliases = {len(args) + 1: 0}
        args += [*in_vmem(before[0]), before[1]]
        in_specs += [WHOLE, ANY]
    out_shape = [jax.ShapeDtypeStruct((shard, columns), BF16), pltpu.VMEM((keys, all_rows), BF16)]
    if last:
        out_shape += [pltpu.VMEM((shard, width), d) for d in (F32, BF16, F32, BF16)]
    else:
        out_shape += [acc]
    return pl.pallas_call(
        functools.partial(attend_kernel, tiles, index),
        out_shape=out_shape,
        in_specs=in_specs,
        out_specs=[ANY] + [WHOLE] * (len(out_shape) - 1),
        scratch_shapes=[
            *([acc] if last else []),
            pltpu.VMEM((keys, hd), BF16),
            pltpu.VMEM((keys, hd), BF16),
            pltpu.VMEM((hd, keys), BF16),
            pltpu.VMEM((keys, all_rows), BF16),
            pltpu.VMEM((rows, columns), BF16),
            pltpu.SemaphoreType.DMA((columns // hd // HEADS,)),
        ],
        input_output_aliases=aliases,
        compiler_params=params(24),
        cost_estimate=pl.CostEstimate(
            flops=10 * keys * rows * columns, transcendentals=keys * all_rows, bytes_accessed=1 << 21
        ),
        name="attend_last" if last else "attend_first",
    )(*args)


def query_gradients(shards, dscores, columns):
    shard, width = shards[0].shape
    tiles = len(dscores)
    hd, keys = width // 2, dscores[0].shape[0]
    return pl.pallas_call(
        functools.partial(queries_kernel, tiles),
        out_shape=jax.ShapeDtypeStruct((shard, columns), BF16),
        in_specs=[WHOLE] * (WIN + tiles),
        out_specs=ANY,
        scratch_shapes=[
            pltpu.VMEM((keys, hd), BF16),
            pltpu.VMEM((hd, keys), BF16),
            pltpu.VMEM((shard, columns), BF16),
            pltpu.SemaphoreType.DMA((tiles * (columns // hd // HEADS),)),
        ],
        compiler_params=params(12),
        cost_estimate=pl.CostEstimate(flops=2 * keys * shard * columns, transcendentals=0, bytes_accessed=1 << 21),
        name="query_gradients",
    )(*in_vmem(*shards, *dscores))


def gather_kernel(own_ref, *refs):
    total = own_ref[...]
    for r in refs[:-2]:
        total = total + r[...].astype(F32)
    hd = refs[-1].shape[1]
    refs[-2][...] = total[:, :hd].astype(BF16)
    refs[-1][...] = total[:, hd:].astype(BF16)


def in_order_kernel(own_ref, *refs):
    info = place()
    near, (k_ref, v_ref) = refs[:-2], refs[-2:]
    shard, hd = k_ref.shape
    part = shard // 2
    total = own_ref[...]
    for r in near:
        total = total + r[...].astype(F32)
    for j in range(2):
        to = pl.ds(pl.multiple_of((j ^ info[1]) * part, part), part)
        k_ref[to, :] = total[j * part : (j + 1) * part, :hd].astype(BF16)
        v_ref[to, :] = total[j * part : (j + 1) * part, hd:].astype(BF16)


def move(value, kind, back=False):
    count = lax.axis_size("ctx")
    steps = {A: lambda i: 3 if i % 2 else 1, B: lambda i: 2, C: lambda i: -1 if i % 2 else 1}[kind]
    pairs = [(i, (i + steps(i)) % count) for i in range(count)]
    return lax.ppermute(value, "ctx", [p[::-1] for p in pairs] if back else pairs)


def window(own, bias):
    a = move(own, A)
    b = move(own, B)
    b, *bias = lax.optimization_barrier((b, *bias))
    return [own, a, b, move(b, C)], bias


def body(queries, keys, values, d_out, doc_lengths):
    count = lax.axis_size("head")
    head = lax.axis_index("head")
    shard = count * queries.shape[0]
    hd = keys.shape[1] // count
    columns = queries.shape[1] // count
    tiles = 2 if count == 2 else 1
    bias = masks(doc_lengths, shard, tiles)
    if tiles == 2:
        other = 1 - head

        def half(x, index):
            width = x.shape[1] // 2
            return lax.dynamic_slice_in_dim(x, index * width, width, 1)

        def key_value(index):
            return jnp.concatenate([half(keys, index), half(values, index)], axis=1)

        def swap(x):
            return lax.ppermute(x, "head", [(0, 1), (1, 0)])

        own = jnp.concatenate([key_value(head), swap(key_value(other))], axis=0)
        both = swap(jnp.concatenate([half(queries, other), half(d_out, other)], axis=1))
        shards, bias = window(own, bias)
        out, ds_first, acc = attend((queries, d_out), bias[0], shards, None, 2, columns)
        out, ds_last, *grads = attend((both,), bias[1], shards, (acc, out), 2, columns)
        dscores = (ds_first, ds_last)
    else:
        swap = lambda x: lax.all_to_all(x, "head", split_axis=1, concat_axis=0, tiled=True)
        own = jnp.concatenate([swap(keys), swap(values)], axis=1)
        both = jnp.concatenate([swap(queries), swap(d_out)], axis=1)
        shards, bias = window(own, bias)
        out, ds_last, *grads = attend((both,), bias[0], shards, None, 1, columns)
        dscores = (ds_last,)
    from_c = move(grads[C], C, True)
    near_a = move(grads[A], A, True)
    near_b = move((grads[B] + from_c.astype(F32)).astype(BF16), B, True)
    dq = query_gradients(shards, dscores, columns)
    grad_keys, grad_values = pl.pallas_call(
        in_order_kernel if tiles == 2 else gather_kernel,
        out_shape=[jax.ShapeDtypeStruct((shard, hd), BF16)] * 2,
        in_specs=[WHOLE] * 3,
        out_specs=[WHOLE] * 2,
        compiler_params=params(4),
        name="gather",
    )(*in_vmem(grads[OWN], near_a, near_b))
    return out, dq, grad_keys, grad_values


def solution(mesh):
    rows = P(("ctx", "head"), None)
    return jax.shard_map(
        body,
        mesh=mesh,
        in_specs=(rows, rows, rows, rows, P()),
        out_specs=(P("ctx", "head"),) * 4,
        check_vma=False,
    )
```
